256 devices in a mesh: region: 32 (over x, z), comm: 8 (over y, core).
Axes of the slice: x: 4, y: 4, z: 8, core: 2. Of those that a mesh axis runs over, the one named last changes fastest.
Arguments:
- cost: float32 [128, 262144], P('comm', 'region'), may hold values from 0.01 to 15, as said below
- flow_start: float32 [128, 262144], P('comm', 'region'), may hold values from 0 to 0.5
- capacity: float32 [262144], P('region'), may hold values from 5 to 135, as said below
- cap_dual_start: float32 [262144], P('region'), may hold values from 0 to 1
- demand: float32 [128, 131072], P('comm', 'region'), may hold values from -24 to 24
- node_dual_start: float32 [128, 131072], P('comm', 'region'), may hold values from -6 to 6
- incidence: float32 [4096, 128, 128], P('region'), may hold values from -0.25 to 0.25
- block_node: int32 [4096], P('region'), may hold values from 0 to 39
- ghost_source: int32 [256], P('region'), may hold values from 0 to 127, as said below
Outputs:
- final_flow: float32 [128, 262144], P('comm', 'region')
- final_cap_dual: float32 [262144], P('region')
- final_node_dual: float32 [128, 131072], P('comm', 'region')
The draws below stay inside these ranges and needn't reach their ends.
Inputs may be any that keep to these rules, and one draw needn't show every extreme that they name: Each cost is positive. Each capacity is positive. `ghost_source`: ghost slot g of region r names boundary block j of region q as q * 4 + j. Slot 0 of every region has q = r + 16 in cyclic order; every other slot has q at most two regions from r in cyclic order (q may be r).
All inputs are finite; a program needn't handle non-finite values.
Results may differ from the reference program's by a relative error of at most 0.00021.
Values sent between devices are 32-bit elements; how exact they have to be, the bound alone decides.
A program may use at most 64 MiB of HBM per device.

```python
import jax
import jax.numpy as jnp
from jax import lax

K = 128
BLK = 128
AB = 64
BPA = 2
NBD = 4
NG = 8
ITERS = 2
NODE_BLK = 32
ARCS = 262144
NODES = 131072
NBLK_ALL = 4096
GHOSTS = 256
BOUND = 128
N_REGION = 32


def draw_cost(key, part):
    row_frac = jnp.arange(K, dtype=jnp.float32)[:, None] / K
    col_frac = jnp.arange(ARCS, dtype=jnp.float32)[None, :] / ARCS
    scales = jnp.power(10.0, row_frac + col_frac)
    rough = jax.random.uniform(key, (K, ARCS), jnp.float32, 0.5, 1.5)
    return (0.1 * scales * rough).astype(jnp.float32)


def draw_capacity(key, part):
    col_frac = jnp.arange(ARCS, dtype=jnp.float32) / ARCS
    rough = jax.random.uniform(key, (ARCS,), jnp.float32, 0.75, 1.25)
    return (20.0 * (1.0 + 2.0 * col_frac) * rough).astype(jnp.float32)


def draw_ghost_source(key, part):
    key_offset, key_block = jax.random.split(jax.random.fold_in(key, 7))
    region_count = BOUND // NBD
    slot_ids = jnp.arange(GHOSTS, dtype=jnp.int32)
    home_region = slot_ids // NG
    offset_draw = jax.random.randint(key_offset, (GHOSTS,), -2, 3).astype(jnp.int32)
    far_offset = jnp.full((GHOSTS,), region_count // 2, dtype=jnp.int32)
    offset_used = jnp.where(slot_ids % NG == 0, far_offset, offset_draw).astype(jnp.int32)
    owner_region = (home_region + offset_used + 2 * region_count) % region_count
    block_pick = jax.random.randint(key_block, (GHOSTS,), 0, NBD).astype(jnp.int32)
    return (owner_region * NBD + block_pick).astype(jnp.int32)


def touch_ends(values, rng, least, largest):
    longest = values.shape.index(max(values.shape))
    spots = []
    for shift in (0, 1):
        where = [jax.random.randint(jax.random.fold_in(rng, axis), (), 0, length) for axis, length in enumerate(values.shape)]
        where[longest] = (where[longest] + shift) % values.shape[longest]
        spots.append(tuple(where))
    return values.at[spots[0]].set(least).at[spots[1]].set(largest)


def steps_of(stream_key, extent, shards, least, largest):
    loudness, own = 1.0, jax.random.fold_in(stream_key, 6)
    for position, parts in shards:
        draws = jnp.exp(jax.random.uniform(jax.random.fold_in(own, position), (parts,), jnp.float32, least / len(shards), largest / len(shards)))
        loudness = loudness * jnp.repeat(draws, extent[position] // parts).reshape([-1 if axis == position else 1 for axis in range(len(extent))])
    return loudness


def noise(stream_key, dims, width, bound, shards=(), kind=jnp.bfloat16):
    array = width * jax.random.normal(stream_key, dims, jnp.float32)
    if shards:
        array = array * steps_of(stream_key, dims, shards, -0.22, 0.18)
    return jnp.clip(array, -bound, bound).astype(kind)


def setup_inputs(seed: int = 0) -> dict:
    streams_of = jax.random.split(jax.random.key(seed), 10)
    return {
        "cost": draw_cost(jax.random.fold_in(streams_of[9], 71), 0),
        "flow_start": jnp.clip(0.5 * jax.random.uniform(streams_of[1], (K, ARCS), jnp.float32) ** steps_of(streams_of[1], (K, ARCS), ((0, 8), (1, 32)), -0.2, 0.2), 0.0, 0.5),
        "capacity": draw_capacity(jax.random.fold_in(streams_of[9], 71), 0),
        "cap_dual_start": jnp.clip(1.0 * jax.random.uniform(streams_of[3], (ARCS,), jnp.float32) ** steps_of(streams_of[3], (ARCS,), ((0, 32),), -0.2, 0.2), 0.0, 1.0),
        "demand": noise(streams_of[4], (K, NODES), 4.0, 24.0, ((0, 8), (1, 32)), jnp.float32),
        "node_dual_start": noise(streams_of[5], (K, NODES), 1.0, 6.0, ((0, 8), (1, 32)), jnp.float32),
        "incidence": noise(streams_of[6], (NBLK_ALL, BLK, BLK), (4 * BLK) ** -0.5, 0.25, ((0, 32),), jnp.float32),
        "block_node": touch_ends(jax.random.randint(streams_of[7], (NBLK_ALL,), 0, NODE_BLK + NG), jax.random.fold_in(streams_of[7], 1), 0, (NODE_BLK + NG) - 1).astype(jnp.int32),
        "ghost_source": draw_ghost_source(jax.random.fold_in(streams_of[9], 71), 0),
    }


step_scale = 0.08
highest = lax.Precision.HIGHEST

def reference(cost, flow_start, capacity, cap_dual_start, demand, node_dual_start, incidence, block_node, ghost_source):
    block_count = AB * BPA * N_REGION
    region_of = jnp.arange(block_count, dtype=jnp.int32) // (AB * BPA)
    ghost_slot = jnp.clip(block_node - NODE_BLK, 0, NG - 1).astype(jnp.int32)
    bound_index = ghost_source[region_of * NG + ghost_slot]
    ghost_block = bound_index // NBD * NODE_BLK + bound_index % NBD
    owned_block = region_of * NODE_BLK + block_node
    node_block = jnp.where(block_node < NODE_BLK, owned_block, ghost_block).astype(jnp.int32)
    weight = jnp.sqrt(jnp.sum(cost * cost) / (jnp.sum(demand * demand) + jnp.sum(capacity * capacity)))
    primal_step = step_scale / weight
    dual_step = step_scale * weight
    flow_now, cap_dual, node_dual = (flow_start, cap_dual_start, node_dual_start)
    for iteration in range(ITERS):
        chosen_duals = node_dual.reshape(K, NODES // BLK, BLK)[:, node_block]
        back_term = jnp.einsum('kbn,bna->kba', chosen_duals, incidence, precision=highest)
        back_term = back_term.reshape(K, block_count // BPA, BPA, BLK).sum(axis=2).reshape(K, ARCS)
        flow_new = jnp.maximum(flow_now - primal_step * (cost - back_term + cap_dual[None, :]), 0.0)
        flow_bar = 2.0 * flow_new - flow_now
        arc_load = lax.optimization_barrier(jnp.sum(flow_bar, axis=0))
        cap_dual = jnp.maximum(cap_dual + dual_step * (arc_load - capacity), 0.0)
        repeated_flow = jnp.repeat(flow_bar.reshape(K, ARCS // BLK, BLK), BPA, axis=1)
        forward = jnp.einsum('kba,bna->bkn', repeated_flow, incidence, precision=highest)
        node_rows = jax.ops.segment_sum(forward, node_block, num_segments=NODES // BLK)
        node_rows = jnp.transpose(node_rows, (1, 0, 2)).reshape(K, NODES)
        node_dual = node_dual + dual_step * (demand - node_rows)
        flow_now = flow_new
    return (flow_now, cap_dual, node_dual)
```

```python
import functools

import jax
import jax.numpy as jnp
from jax import lax
from jax.experimental import pallas as pl
from jax.experimental.pallas import tpu as pltpu
from jax.sharding import PartitionSpec as P

BPA = 2
NBD = 4
NG = 8
ITERS = 2
BLK = 128
Z_SIZE = 8
CHUNKS = 8
UNROLL = 8
ROW_PAD = 64

step_scale = 0.08
MESH = pl.DeviceIdType.MESH


def split(value):
    high = value.astype(jnp.bfloat16)
    low = (value - high.astype(jnp.float32)).astype(jnp.bfloat16)
    return high, low


def columns(block):
    if isinstance(block, int):
        return pl.ds(block * BLK, BLK)
    return pl.ds(pl.multiple_of(block * BLK, BLK), BLK)


def square_sum(ref, width):
    def step(index, total):
        for part in range(4):
            piece = ref[:, columns(index * 4 + part)]
            squares = piece * piece
            total = total + (squares[:8] + squares[8:])
        return total

    return lax.fori_loop(0, width // (4 * BLK), step, jnp.zeros((8, BLK), jnp.float32))


def kernel(
    regions,
    comms,
    bn,
    gs,
    bn_row,
    cost,
    flow,
    capacity,
    cap_dual,
    demand,
    node_dual,
    inc_hbm,
    flow_o,
    cap_o,
    nd_o,
    inc_buf,
    w2,
    back_s,
    nd3,
    dtab,
    oh2,
    cand,
    fwd,
    slot,
    rbuf,
    load_s,
    ld_a,
    ld_b,
    sbuf,
    inc_sem,
    sc_send,
    sc_recv,
    gh_send,
    gh_recv,
    rt_send,
    rt_recv,
    ld_send,
    ld_recv,
):
    r = lax.axis_index("region")
    c = lax.axis_index("comm")
    own = nd3.shape[0]
    arc_blocks = w2.shape[0]
    commodities = cost.shape[0]
    x_size = regions // Z_SIZE
    x = r // Z_SIZE
    z = lax.rem(r, Z_SIZE)
    deltas = (1, 2, regions - 2, regions - 1, regions // 2)
    per_chunk = inc_buf.shape[0] // CHUNKS
    load_rows = load_s.shape[0] // comms

    inc_copies = []
    for chunk in range(CHUNKS):
        rows = pl.ds(chunk * per_chunk, per_chunk)
        copy = pltpu.make_async_copy(inc_hbm.at[rows], inc_buf.at[rows], inc_sem.at[chunk])
        copy.start()
        inc_copies.append(copy)

    def comm_peer(off):
        return {"region": r, "comm": lax.rem(c + off, comms)}

    def x_peer(off):
        return {"region": lax.rem(x + off, x_size) * Z_SIZE + z, "comm": c}

    def z_peer(off):
        return {"region": x * Z_SIZE + lax.rem(z + off, Z_SIZE), "comm": c}

    def r_peer(off):
        return {"region": lax.rem(r + off, regions), "comm": c}

    barrier = pltpu.get_barrier_semaphore()
    greeted = 0
    for peer, offs in (
        (comm_peer, range(1, comms)),
        (x_peer, range(1, x_size)),
        (z_peer, range(1, Z_SIZE)),
        (r_peer, deltas[:4]),
    ):
        for off in offs:
            pl.semaphore_signal(barrier, inc=1, device_id=peer(off), device_id_type=MESH)
            greeted += 1

    def spread(index, carry):
        for part in range(4):
            s = index * 4 + part
            value = node_dual[:, columns(s)]
            nd3[s] = value
            high, low = split(value)
            dtab[s, 0:commodities] = high
            dtab[s, commodities:] = low
        return carry

    lax.fori_loop(0, own // 4, spread, 0)
    for j in range(NBD):
        cand[j] = node_dual[:, columns(j)]

    sbuf[0, c, 0:8] = square_sum(cost, cost.shape[1])
    sbuf[0, c, 8:16] = square_sum(demand, demand.shape[1])

    ghost_at = []
    code = bn_row[...]
    slots = code
    for g in range(NG):
        source = gs[g]
        block = source & (NBD - 1)
        delta = lax.rem((source >> 2) - r + regions, regions)
        behind = jnp.maximum(delta - (regions - 5), 3)
        relation = jnp.where(delta <= 2, delta, jnp.where(delta == regions // 2, 5, behind))
        ghost_at.append(relation * NBD + block)
        row = jnp.where(relation == 0, block, own - NBD + relation * NBD + block)
        code = jnp.where(slots == own + g, row, code)
    hits = lax.broadcasted_iota(jnp.int32, (ROW_PAD, BLK), 0) == code
    one_hot = jnp.where(hits, 1.0, 0.0).astype(jnp.bfloat16)
    oh2[:, 0:BLK] = one_hot
    oh2[:, BLK:] = one_hot

    pl.semaphore_wait(barrier, greeted)

    def send_scalars(stage, peer, count, me):
        copies = []
        for off in range(1, count):
            copy = pltpu.make_async_remote_copy(
                src_ref=sbuf.at[stage, me],
                dst_ref=sbuf.at[stage, me],
                send_sem=sc_send.at[stage, off],
                recv_sem=sc_recv.at[stage, off],
                device_id=peer(off),
                device_id_type=MESH,
            )
            copy.start()
            copies.append(copy)
        return copies

    def take_scalars(stage, copies):
        for copy in copies:
            copy.wait()
        total = sbuf[stage, 0]
        for index in range(1, len(copies) + 1):
            total = total + sbuf[stage, index]
        return total

    def send_ghosts(it):
        copies = []
        for index, delta in enumerate(deltas):
            copy = pltpu.make_async_remote_copy(
                src_ref=nd3.at[pl.ds(0, NBD)],
                dst_ref=cand.at[pl.ds(it * 24 + (index + 1) * NBD, NBD)],
                send_sem=gh_send.at[it, index],
                recv_sem=gh_recv.at[it, index],
                device_id=r_peer(regions - delta),
                device_id_type=MESH,
            )
            copy.start()
            copies.append(copy)
        return copies

    def convert(chunk):
        inc_copies[chunk].wait()
        blocks = arc_blocks // CHUNKS

        def step(index, carry):
            a = chunk * blocks + index
            for b in range(BPA):
                high, low = split(inc_buf[a * BPA + b])
                w2[a, b * BLK : (b + 1) * BLK, 0:BLK] = high
                w2[a, b * BLK : (b + 1) * BLK, BLK:] = low
            return carry

        lax.fori_loop(0, blocks, step, 0)

    ghost_copies = send_ghosts(0)
    scalar_copies = send_scalars(0, comm_peer, comms, c)
    for chunk in range(0, 3):
        convert(chunk)
    total = take_scalars(0, scalar_copies)
    cap_sq = jnp.zeros((8, BLK), jnp.float32)
    for part in range(capacity.shape[0] // 8):
        piece = capacity[part * 8 : (part + 1) * 8]
        cap_sq = cap_sq + piece * piece
    sbuf[1, x, 0:8] = total[0:8]
    sbuf[1, x, 8:16] = total[8:16] + cap_sq
    convert(3)
    scalar_copies = send_scalars(1, x_peer, x_size, x)
    for chunk in range(4, 7):
        convert(chunk)
    total = take_scalars(1, scalar_copies)
    sbuf[2, z] = total
    convert(7)
    scalar_copies = send_scalars(2, z_peer, Z_SIZE, z)

    primal_step = None
    dual_step = None
    for it in range(ITERS):
        last = it == ITERS - 1
        flow_src = flow if it == 0 else flow_o
        cap_src = cap_dual if it == 0 else cap_o

        for copy in ghost_copies:
            copy.wait()
        for g in range(NG):
            high, low = split(cand[it * 24 + ghost_at[g]])
            dtab[own + g, 0:commodities] = high
            dtab[own + g, commodities:] = low

        def back_step(index, carry):
            for part in range(UNROLL):
                a = index * UNROLL + part
                left = dtab[bn[a * BPA]]
                right = dtab[bn[a * BPA + 1]]
                product = jnp.dot(
                    jnp.concatenate([left, right], axis=1),
                    w2[a],
                    preferred_element_type=jnp.float32,
                )
                half = product[:commodities] + product[commodities:]
                back_s[:, columns(a)] = half[:, :BLK] + half[:, BLK:]
            return carry

        lax.fori_loop(0, arc_blocks // UNROLL, back_step, 0)

        if it == 0:
            total = take_scalars(2, scalar_copies)
            cost_all = jnp.sum(total[0:8], axis=(0, 1), keepdims=True)
            rest_all = jnp.sum(total[8:16], axis=(0, 1), keepdims=True)
            weight = jnp.sqrt(cost_all / rest_all)
            primal_step = jnp.broadcast_to(step_scale / weight, (1, BLK))
            dual_step = jnp.broadcast_to(step_scale * weight, (1, BLK))
        else:
            finish_load(it - 1)

        def flow_step(index, carry):
            for part in range(UNROLL):
                a = index * UNROLL + part
                now = flow_src[:, columns(a)]
                price = cost[:, columns(a)] - back_s[:, columns(a)] + cap_src[pl.ds(a, 1), :]
                new = jnp.maximum(now - primal_step * price, 0.0)
                bar = 2.0 * new - now
                flow_o[:, columns(a)] = new
                load_s[pl.ds(a, 1), :] = jnp.sum(bar, axis=0, keepdims=True)
                high, low = split(bar)
                terms = jnp.concatenate(
                    [
                        jnp.concatenate([high, high], axis=1),
                        jnp.concatenate([low, low], axis=1),
                    ],
                    axis=0,
                )
                product = lax.dot_general(
                    terms,
                    w2[a],
                    (((1,), (1,)), ((), ())),
                    preferred_element_type=jnp.float32,
                )
                half = product[:commodities] + product[commodities:]
                row = pl.multiple_of(a * (BPA * commodities), BPA * commodities)
                fwd[pl.ds(row, commodities), :] = half[:, :BLK]
                fwd[pl.ds(row + commodities, commodities), :] = half[:, BLK:]
            return carry

        lax.fori_loop(0, arc_blocks // UNROLL, flow_step, 0)

        load_copies = []
        blocks = BPA * arc_blocks
        for pair in range(commodities // 2):
            high_0, low_0 = split(fwd[pl.ds(2 * pair, blocks, stride=commodities), :])
            high_1, low_1 = split(fwd[pl.ds(2 * pair + 1, blocks, stride=commodities), :])
            terms = jnp.concatenate(
                [
                    jnp.concatenate([high_0, high_1], axis=1),
                    jnp.concatenate([low_0, low_1], axis=1),
                ],
                axis=0,
            )
            rows = jnp.dot(oh2[...], terms, preferred_element_type=jnp.float32)
            slot[pl.ds(2 * pair, ROW_PAD, stride=commodities), :] = rows[:, :BLK]
            slot[pl.ds(2 * pair + 1, ROW_PAD, stride=commodities), :] = rows[:, BLK:]
            if pair == 0:
                for off in range(1, comms):
                    target = lax.rem(c + off, comms)
                    copy = pltpu.make_async_remote_copy(
                        src_ref=load_s.at[
                            pl.ds(pl.multiple_of(target * load_rows, load_rows), load_rows)
                        ],
                        dst_ref=ld_a.at[it, c],
                        send_sem=ld_send.at[it, 0, off],
                        recv_sem=ld_recv.at[it, 0, off],
                        device_id=comm_peer(off),
                        device_id_type=MESH,
                    )
                    copy.start()
                    load_copies.append(copy)

        for copy in load_copies:
            copy.wait()
        mine = load_s[pl.ds(pl.multiple_of(c * load_rows, load_rows), load_rows), :]
        for off in range(1, comms):
            mine = mine + ld_a[it, lax.rem(c + off, comms)]
        ld_b[it, c] = mine

        routed_copies = []
        for index, delta in enumerate(deltas):
            rows = NBD * commodities
            copy = pltpu.make_async_remote_copy(
                src_ref=slot.at[pl.ds(own * commodities + index * rows, rows)],
                dst_ref=rbuf.at[it, index],
                send_sem=rt_send.at[it, index],
                recv_sem=rt_recv.at[it, index],
                device_id=r_peer(delta),
                device_id_type=MESH,
            )
            copy.start()
            routed_copies.append(copy)

        total_copies = []
        for off in range(1, comms):
            copy = pltpu.make_async_remote_copy(
                src_ref=ld_b.at[it, c],
                dst_ref=ld_b.at[it, c],
                send_sem=ld_send.at[it, 1, off],
                recv_sem=ld_recv.at[it, 1, off],
                device_id=comm_peer(off),
                device_id_type=MESH,
            )
            copy.start()
            total_copies.append(copy)

        def finish_load(at, copies=total_copies, source=cap_src):
            for copy in copies:
                copy.wait()
            for owner in range(comms):
                rows = slice(owner * load_rows, (owner + 1) * load_rows)
                excess = ld_b[at, owner] - capacity[rows]
                cap_o[rows] = jnp.maximum(source[rows] + dual_step * excess, 0.0)

        def updated(s, rows):
            return nd3[s] + dual_step * (demand[:, columns(s)] - rows)

        def keep(s, value):
            if last:
                nd_o[:, columns(s)] = value
            else:
                nd3[s] = value
                high, low = split(value)
                dtab[s, 0:commodities] = high
                dtab[s, commodities:] = low

        def inner_step(index, carry):
            for part in range(4):
                s = NBD + index * 4 + part
                row = pl.multiple_of(s * commodities, commodities)
                keep(s, updated(s, slot[pl.ds(row, commodities), :]))
            return carry

        lax.fori_loop(0, (own - NBD) // 4, inner_step, 0)

        for copy in routed_copies:
            copy.wait()
        for j in range(NBD):
            rows = slot[j * commodities : (j + 1) * commodities, :]
            for index in range(len(deltas)):
                rows = rows + rbuf[it, index, j * commodities : (j + 1) * commodities, :]
            value = updated(j, rows)
            keep(j, value)
            if not last:
                cand[(it + 1) * 24 + j] = value
        if last:
            finish_load(it)
        else:
            ghost_copies = send_ghosts(it + 1)


def body(
    cost,
    flow_start,
    capacity,
    cap_dual_start,
    demand,
    node_dual_start,
    incidence,
    block_node,
    ghost_source,
):
    regions = lax.axis_size("region")
    comms = lax.axis_size("comm")
    commodities, arcs = cost.shape
    nodes = demand.shape[1]
    arc_blocks = arcs // BLK
    own = nodes // BLK
    blocks = incidence.shape[0]
    f32, bf16 = jnp.float32, jnp.bfloat16
    vmem = pl.BlockSpec(memory_space=pltpu.VMEM)
    smem = pl.BlockSpec(memory_space=pltpu.SMEM)
    dma = pltpu.SemaphoreType.DMA
    relations = 5
    flow_end, cap_end, node_end = pl.pallas_call(
        functools.partial(kernel, regions, comms),
        name="pdhg",
        out_shape=(
            jax.ShapeDtypeStruct((commodities, arcs), f32),
            jax.ShapeDtypeStruct((arc_blocks, BLK), f32),
            jax.ShapeDtypeStruct((commodities, nodes), f32),
        ),
        in_specs=[smem, smem] + [vmem] * 7 + [pl.BlockSpec(memory_space=pl.ANY)],
        out_specs=(vmem, vmem, vmem),
        scratch_shapes=[
            pltpu.VMEM((blocks, BLK, BLK), f32),
            pltpu.VMEM((arc_blocks, BPA * BLK, 2 * BLK), bf16),
            pltpu.VMEM((commodities, arcs), f32),
            pltpu.VMEM((own, commodities, BLK), f32),
            pltpu.VMEM((own + NG, 2 * commodities, BLK), bf16),
            pltpu.VMEM((ROW_PAD, 2 * BLK), bf16),
            pltpu.VMEM((ITERS * 24, commodities, BLK), f32),
            pltpu.VMEM((blocks * commodities, BLK), f32),
            pltpu.VMEM((ROW_PAD * commodities, BLK), f32),
            pltpu.VMEM((ITERS, relations, NBD * commodities, BLK), f32),
            pltpu.VMEM((arc_blocks, BLK), f32),
            pltpu.VMEM((ITERS, comms, arc_blocks // comms, BLK), f32),
            pltpu.VMEM((ITERS, comms, arc_blocks // comms, BLK), f32),
            pltpu.VMEM((3, 8, 16, BLK), f32),
            dma((CHUNKS,)),
            dma((3, 8)),
            dma((3, 8)),
            dma((ITERS, relations)),
            dma((ITERS, relations)),
            dma((ITERS, relations)),
            dma((ITERS, relations)),
            dma((ITERS, 2, 8)),
            dma((ITERS, 2, 8)),
        ],
        compiler_params=pltpu.CompilerParams(
            collective_id=0, has_side_effects=True, vmem_limit_bytes=50 * 1024 * 1024
        ),
    )(
        block_node,
        ghost_source,
        block_node.reshape(1, blocks),
        cost,
        flow_start,
        capacity.reshape(arc_blocks, BLK),
        cap_dual_start.reshape(arc_blocks, BLK),
        demand,
        node_dual_start,
        incidence,
    )
    return flow_end, cap_end.reshape(arcs), node_end


def solution(mesh):
    return jax.shard_map(
        body,
        mesh=mesh,
        in_specs=(
            P("comm", "region"),
            P("comm", "region"),
            P("region"),
            P("region"),
            P("comm", "region"),
            P("comm", "region"),
            P("region", None, None),
            P("region"),
            P("region"),
        ),
        out_specs=(P("comm", "region"), P("region"), P("comm", "region")),
        check_vma=False,
    )
```

```python
import functools

import jax
import jax.numpy as jnp
from jax import lax
from jax.experimental import pallas as pl
from jax.experimental.pallas import tpu as pltpu
from jax.sharding import PartitionSpec as P

BPA = 2
NBD = 4
NG = 8
ITERS = 2
BLK = 128
Z_SIZE = 8
CHUNKS = 8
UNROLL = 8
ROW_PAD = 64

step_scale = 0.08
MESH = pl.DeviceIdType.MESH


def split(value):
    high = value.astype(jnp.bfloat16)
    low = (value - high.astype(jnp.float32)).astype(jnp.bfloat16)
    return high, low


def columns(block):
    if isinstance(block, int):
        return pl.ds(block * BLK, BLK)
    return pl.ds(pl.multiple_of(block * BLK, BLK), BLK)


def square_sum(ref, width):
    def step(index, total):
        for part in range(4):
            piece = ref[:, columns(index * 4 + part)]
            squares = piece * piece
            total = total + (squares[:8] + squares[8:])
        return total

    return lax.fori_loop(0, width // (4 * BLK), step, jnp.zeros((8, BLK), jnp.float32))


def kernel(
    regions,
    comms,
    bn_hbm,
    gs_hbm,
    bn_row_hbm,
    cost_hbm,
    flow_hbm,
    capacity_hbm,
    cap_dual_hbm,
    demand_hbm,
    node_dual_hbm,
    inc_hbm,
    flow_hbm_o,
    cap_hbm_o,
    nd_hbm_o,
    flow_o,
    cap_o,
    nd_o,
    bn,
    gs,
    bn_row,
    cost,
    flow,
    capacity,
    cap_dual,
    demand,
    node_dual,
    inc_buf,
    w2,
    back_s,
    nd3,
    dtab,
    oh2,
    cand,
    fwd,
    slot,
    rbuf,
    load_s,
    ld_a,
    ld_b,
    sbuf,
    out_sem,
    arg_sem,
    inc_sem,
    sc_send,
    sc_recv,
    gh_send,
    gh_recv,
    rt_send,
    rt_recv,
    ld_send,
    ld_recv,
):
    r = lax.axis_index("region")
    c = lax.axis_index("comm")
    own = nd3.shape[0]
    arc_blocks = w2.shape[0]
    commodities = cost.shape[0]
    x_size = regions // Z_SIZE
    x = r // Z_SIZE
    z = lax.rem(r, Z_SIZE)
    deltas = (1, 2, regions - 2, regions - 1, regions // 2)
    per_chunk = inc_buf.shape[0] // CHUNKS
    load_rows = load_s.shape[0] // comms

    arg_copies = {}
    for index, (name, source, target) in enumerate(
        (
            ("cost", cost_hbm, cost),
            ("node_dual", node_dual_hbm, node_dual),
            ("demand", demand_hbm, demand),
            ("gs", gs_hbm, gs),
            ("bn_row", bn_row_hbm, bn_row),
            ("bn", bn_hbm, bn),
            ("capacity", capacity_hbm, capacity),
            ("cap_dual", cap_dual_hbm, cap_dual),
            ("flow", flow_hbm, flow),
        )
    ):
        copy = pltpu.make_async_copy(source, target, arg_sem.at[index])
        copy.start()
        arg_copies[name] = copy
    out_copies = []

    def put_out(index, source, target):
        copy = pltpu.make_async_copy(source, target, out_sem.at[index])
        copy.start()
        out_copies.append(copy)

    inc_copies = []
    for chunk in range(CHUNKS):
        rows = pl.ds(chunk * per_chunk, per_chunk)
        copy = pltpu.make_async_copy(inc_hbm.at[rows], inc_buf.at[rows], inc_sem.at[chunk])
        copy.start()
        inc_copies.append(copy)

    def comm_peer(off):
        return {"region": r, "comm": lax.rem(c + off, comms)}

    def x_peer(off):
        return {"region": lax.rem(x + off, x_size) * Z_SIZE + z, "comm": c}

    def z_peer(off):
        return {"region": x * Z_SIZE + lax.rem(z + off, Z_SIZE), "comm": c}

    def r_peer(off):
        return {"region": lax.rem(r + off, regions), "comm": c}

    barrier = pltpu.get_barrier_semaphore()
    greeted = 0
    for peer, offs in (
        (comm_peer, range(1, comms)),
        (x_peer, range(1, x_size)),
        (z_peer, range(1, Z_SIZE)),
        (r_peer, deltas[:4]),
    ):
        for off in offs:
            pl.semaphore_signal(barrier, inc=1, device_id=peer(off), device_id_type=MESH)
            greeted += 1

    def spread(index, carry):
        for part in range(4):
            s = index * 4 + part
            value = node_dual[:, columns(s)]
            nd3[s] = value
            high, low = split(value)
            dtab[s, 0:commodities] = high
            dtab[s, commodities:] = low
        return carry

    arg_copies["node_dual"].wait()
    lax.fori_loop(0, own // 4, spread, 0)
    for j in range(NBD):
        cand[j] = node_dual[:, columns(j)]

    arg_copies["cost"].wait()
    sbuf[0, c, 0:8] = square_sum(cost, cost.shape[1])
    arg_copies["demand"].wait()
    sbuf[0, c, 8:16] = square_sum(demand, demand.shape[1])

    arg_copies["gs"].wait()
    arg_copies["bn_row"].wait()
    ghost_at = []
    code = bn_row[...]
    slots = code
    for g in range(NG):
        source = gs[g]
        block = source & (NBD - 1)
        delta = lax.rem((source >> 2) - r + regions, regions)
        behind = jnp.maximum(delta - (regions - 5), 3)
        relation = jnp.where(delta <= 2, delta, jnp.where(delta == regions // 2, 5, behind))
        ghost_at.append(relation * NBD + block)
        row = jnp.where(relation == 0, block, own - NBD + relation * NBD + block)
        code = jnp.where(slots == own + g, row, code)
    hits = lax.broadcasted_iota(jnp.int32, (ROW_PAD, BLK), 0) == code
    one_hot = jnp.where(hits, 1.0, 0.0).astype(jnp.bfloat16)
    oh2[:, 0:BLK] = one_hot
    oh2[:, BLK:] = one_hot

    pl.semaphore_wait(barrier, greeted)

    def send_scalars(stage, peer, count, me):
        copies = []
        for off in range(1, count):
            copy = pltpu.make_async_remote_copy(
                src_ref=sbuf.at[stage, me],
                dst_ref=sbuf.at[stage, me],
                send_sem=sc_send.at[stage, off],
                recv_sem=sc_recv.at[stage, off],
                device_id=peer(off),
                device_id_type=MESH,
            )
            copy.start()
            copies.append(copy)
        return copies

    def take_scalars(stage, copies):
        for copy in copies:
            copy.wait()
        total = sbuf[stage, 0]
        for index in range(1, len(copies) + 1):
            total = total + sbuf[stage, index]
        return total

    def send_ghosts(it):
        copies = []
        for index, delta in enumerate(deltas):
            copy = pltpu.make_async_remote_copy(
                src_ref=nd3.at[pl.ds(0, NBD)],
                dst_ref=cand.at[pl.ds(it * 24 + (index + 1) * NBD, NBD)],
                send_sem=gh_send.at[it, index],
                recv_sem=gh_recv.at[it, index],
                device_id=r_peer(regions - delta),
                device_id_type=MESH,
            )
            copy.start()
            copies.append(copy)
        return copies

    def convert(chunk):
        inc_copies[chunk].wait()
        blocks = arc_blocks // CHUNKS

        def step(index, carry):
            a = chunk * blocks + index
            for b in range(BPA):
                high, low = split(inc_buf[a * BPA + b])
                w2[a, b * BLK : (b + 1) * BLK, 0:BLK] = high
                w2[a, b * BLK : (b + 1) * BLK, BLK:] = low
            return carry

        lax.fori_loop(0, blocks, step, 0)

    ghost_copies = send_ghosts(0)
    scalar_copies = send_scalars(0, comm_peer, comms, c)
    for chunk in range(0, 3):
        convert(chunk)
    total = take_scalars(0, scalar_copies)
    arg_copies["capacity"].wait()
    cap_sq = jnp.zeros((8, BLK), jnp.float32)
    for part in range(capacity.shape[0] // 8):
        piece = capacity[part * 8 : (part + 1) * 8]
        cap_sq = cap_sq + piece * piece
    sbuf[1, x, 0:8] = total[0:8]
    sbuf[1, x, 8:16] = total[8:16] + cap_sq
    convert(3)
    scalar_copies = send_scalars(1, x_peer, x_size, x)
    for chunk in range(4, 7):
        convert(chunk)
    total = take_scalars(1, scalar_copies)
    sbuf[2, z] = total
    convert(7)
    scalar_copies = send_scalars(2, z_peer, Z_SIZE, z)

    arg_copies["bn"].wait()
    arg_copies["cap_dual"].wait()
    arg_copies["flow"].wait()

    primal_step = None
    dual_step = None
    for it in range(ITERS):
        last = it == ITERS - 1
        flow_src = flow if it == 0 else flow_o
        cap_src = cap_dual if it == 0 else cap_o

        for copy in ghost_copies:
            copy.wait()
        for g in range(NG):
            high, low = split(cand[it * 24 + ghost_at[g]])
            dtab[own + g, 0:commodities] = high
            dtab[own + g, commodities:] = low

        def back_of(a):
            left = dtab[bn[a * BPA]]
            right = dtab[bn[a * BPA + 1]]
            product = jnp.dot(
                jnp.concatenate([left, right], axis=1),
                w2[a],
                preferred_element_type=jnp.float32,
            )
            half = product[:commodities] + product[commodities:]
            return half[:, :BLK] + half[:, BLK:]

        def update(a, back):
            now = flow_src[:, columns(a)]
            price = cost[:, columns(a)] - back + cap_src[pl.ds(a, 1), :]
            new = jnp.maximum(now - primal_step * price, 0.0)
            bar = 2.0 * new - now
            flow_o[:, columns(a)] = new
            load_s[pl.ds(a, 1), :] = jnp.sum(bar, axis=0, keepdims=True)
            back_s[:, columns(a)] = bar

        def back_step(index, carry):
            for part in range(UNROLL):
                a = index * UNROLL + part
                back_s[:, columns(a)] = back_of(a)
            return carry

        def update_step(index, carry):
            for part in range(UNROLL):
                a = index * UNROLL + part
                update(a, back_s[:, columns(a)])
            return carry

        def both_step(index, carry):
            for part in range(UNROLL):
                a = index * UNROLL + part
                update(a, back_of(a))
            return carry

        if it == 0:
            lax.fori_loop(0, arc_blocks // UNROLL, back_step, 0)
            total = take_scalars(2, scalar_copies)
            cost_all = jnp.sum(total[0:8], axis=(0, 1), keepdims=True)
            rest_all = jnp.sum(total[8:16], axis=(0, 1), keepdims=True)
            weight = jnp.sqrt(cost_all / rest_all)
            primal_step = jnp.broadcast_to(step_scale / weight, (1, BLK))
            dual_step = jnp.broadcast_to(step_scale * weight, (1, BLK))
            lax.fori_loop(0, arc_blocks // UNROLL, update_step, 0)
        else:
            lax.fori_loop(0, arc_blocks // UNROLL, both_step, 0)

        load_copies = []
        for off in range(1, comms):
            target = lax.rem(c + off, comms)
            copy = pltpu.make_async_remote_copy(
                src_ref=load_s.at[
                    pl.ds(pl.multiple_of(target * load_rows, load_rows), load_rows)
                ],
                dst_ref=ld_a.at[it, c],
                send_sem=ld_send.at[it, 0, off],
                recv_sem=ld_recv.at[it, 0, off],
                device_id=comm_peer(off),
                device_id_type=MESH,
            )
            copy.start()
            load_copies.append(copy)

        def forward_step(index, carry):
            for part in range(UNROLL):
                a = index * UNROLL + part
                high, low = split(back_s[:, columns(a)])
                terms = jnp.concatenate(
                    [
                        jnp.concatenate([high, high], axis=1),
                        jnp.concatenate([low, low], axis=1),
                    ],
                    axis=0,
                )
                product = lax.dot_general(
                    terms,
                    w2[a],
                    (((1,), (1,)), ((), ())),
                    preferred_element_type=jnp.float32,
                )
                half = product[:commodities] + product[commodities:]
                row = pl.multiple_of(a * (BPA * commodities), BPA * commodities)
                fwd[pl.ds(row, commodities), :] = half[:, :BLK]
                fwd[pl.ds(row + commodities, commodities), :] = half[:, BLK:]
            return carry

        lax.fori_loop(0, arc_blocks // UNROLL, forward_step, 0)
        if last:
            put_out(0, flow_o, flow_hbm_o)

        blocks = BPA * arc_blocks
        for pair in range(commodities // 2):
            high_0, low_0 = split(fwd[pl.ds(2 * pair, blocks, stride=commodities), :])
            high_1, low_1 = split(fwd[pl.ds(2 * pair + 1, blocks, stride=commodities), :])
            terms = jnp.concatenate(
                [
                    jnp.concatenate([high_0, high_1], axis=1),
                    jnp.concatenate([low_0, low_1], axis=1),
                ],
                axis=0,
            )
            rows = jnp.dot(oh2[...], terms, preferred_element_type=jnp.float32)
            slot[pl.ds(2 * pair, ROW_PAD, stride=commodities), :] = rows[:, :BLK]
            slot[pl.ds(2 * pair + 1, ROW_PAD, stride=commodities), :] = rows[:, BLK:]

        def updated(s, rows):
            return nd3[s] + dual_step * (demand[:, columns(s)] - rows)

        def keep(s, value):
            if last:
                nd_o[:, columns(s)] = value
            else:
                nd3[s] = value
                high, low = split(value)
                dtab[s, 0:commodities] = high
                dtab[s, commodities:] = low

        def inner_step(index, carry):
            for part in range(4):
                s = NBD + index * 4 + part
                row = pl.multiple_of(s * commodities, commodities)
                keep(s, updated(s, slot[pl.ds(row, commodities), :]))
            return carry

        lax.fori_loop(0, 1, inner_step, 0)

        routed_copies = []
        for index, delta in enumerate(deltas):
            rows = NBD * commodities
            copy = pltpu.make_async_remote_copy(
                src_ref=slot.at[pl.ds(own * commodities + index * rows, rows)],
                dst_ref=rbuf.at[it, index],
                send_sem=rt_send.at[it, index],
                recv_sem=rt_recv.at[it, index],
                device_id=r_peer(delta),
                device_id_type=MESH,
            )
            copy.start()
            routed_copies.append(copy)

        for copy in load_copies:
            copy.wait()
        mine = load_s[pl.ds(pl.multiple_of(c * load_rows, load_rows), load_rows), :]
        for off in range(1, comms):
            mine = mine + ld_a[it, lax.rem(c + off, comms)]
        ld_b[it, c] = mine

        lax.fori_loop(1, (own - NBD) // 4, inner_step, 0)
        inner = pl.ds(NBD * BLK, (own - NBD) * BLK)
        edge = pl.ds(0, NBD * BLK)

        total_copies = []
        for off in range(1, comms):
            copy = pltpu.make_async_remote_copy(
                src_ref=ld_b.at[it, c],
                dst_ref=ld_b.at[it, c],
                send_sem=ld_send.at[it, 1, off],
                recv_sem=ld_recv.at[it, 1, off],
                device_id=comm_peer(off),
                device_id_type=MESH,
            )
            copy.start()
            total_copies.append(copy)

        def finish_load(at, copies=total_copies, source=cap_src):
            for copy in copies:
                copy.wait()
            for owner in range(comms):
                rows = slice(owner * load_rows, (owner + 1) * load_rows)
                excess = ld_b[at, owner] - capacity[rows]
                cap_o[rows] = jnp.maximum(source[rows] + dual_step * excess, 0.0)

        if last:
            put_out(1, nd_o.at[:, inner], nd_hbm_o.at[:, inner])
        for copy in routed_copies:
            copy.wait()
        for j in range(NBD):
            rows = slot[j * commodities : (j + 1) * commodities, :]
            for index in range(len(deltas)):
                rows = rows + rbuf[it, index, j * commodities : (j + 1) * commodities, :]
            value = updated(j, rows)
            keep(j, value)
            if not last:
                cand[(it + 1) * 24 + j] = value
        if last:
            put_out(2, nd_o.at[:, edge], nd_hbm_o.at[:, edge])
            finish_load(it)
            put_out(3, cap_o, cap_hbm_o)
        else:
            ghost_copies = send_ghosts(it + 1)
            finish_load(it)
    for copy in out_copies:
        copy.wait()


def body(
    cost,
    flow_start,
    capacity,
    cap_dual_start,
    demand,
    node_dual_start,
    incidence,
    block_node,
    ghost_source,
):
    regions = lax.axis_size("region")
    comms = lax.axis_size("comm")
    commodities, arcs = cost.shape
    nodes = demand.shape[1]
    arc_blocks = arcs // BLK
    own = nodes // BLK
    blocks = incidence.shape[0]
    f32, bf16 = jnp.float32, jnp.bfloat16
    hbm = pl.BlockSpec(memory_space=pltpu.HBM)
    dma = pltpu.SemaphoreType.DMA
    relations = 5
    flow_end, cap_end, node_end = pl.pallas_call(
        functools.partial(kernel, regions, comms),
        name="pdhg",
        out_shape=(
            jax.ShapeDtypeStruct((commodities, arcs), f32),
            jax.ShapeDtypeStruct((arc_blocks, BLK), f32),
            jax.ShapeDtypeStruct((commodities, nodes), f32),
        ),
        in_specs=[hbm] * 10,
        out_specs=(hbm, hbm, hbm),
        scratch_shapes=[
            pltpu.VMEM((commodities, arcs), f32),
            pltpu.VMEM((arc_blocks, BLK), f32),
            pltpu.VMEM((commodities, nodes), f32),
            pltpu.SMEM((blocks,), jnp.int32),
            pltpu.SMEM((NG,), jnp.int32),
            pltpu.VMEM((1, blocks), jnp.int32),
            pltpu.VMEM((commodities, arcs), f32),
            pltpu.VMEM((commodities, arcs), f32),
            pltpu.VMEM((arc_blocks, BLK), f32),
            pltpu.VMEM((arc_blocks, BLK), f32),
            pltpu.VMEM((commodities, nodes), f32),
            pltpu.VMEM((commodities, nodes), f32),
            pltpu.VMEM((blocks, BLK, BLK), f32),
            pltpu.VMEM((arc_blocks, BPA * BLK, 2 * BLK), bf16),
            pltpu.VMEM((commodities, arcs), f32),
            pltpu.VMEM((own, commodities, BLK), f32),
            pltpu.VMEM((own + NG, 2 * commodities, BLK), bf16),
            pltpu.VMEM((ROW_PAD, 2 * BLK), bf16),
            pltpu.VMEM((ITERS * 24, commodities, BLK), f32),
            pltpu.VMEM((blocks * commodities, BLK), f32),
            pltpu.VMEM((ROW_PAD * commodities, BLK), f32),
            pltpu.VMEM((ITERS, relations, NBD * commodities, BLK), f32),
            pltpu.VMEM((arc_blocks, BLK), f32),
            pltpu.VMEM((ITERS, comms, arc_blocks // comms, BLK), f32),
            pltpu.VMEM((ITERS, comms, arc_blocks // comms, BLK), f32),
            pltpu.VMEM((3, 8, 16, BLK), f32),
            dma((4,)),
            dma((9,)),
            dma((CHUNKS,)),
            dma((3, 8)),
            dma((3, 8)),
            dma((ITERS, relations)),
            dma((ITERS, relations)),
            dma((ITERS, relations)),
            dma((ITERS, relations)),
            dma((ITERS, 2, 8)),
            dma((ITERS, 2, 8)),
        ],
        compiler_params=pltpu.CompilerParams(
            collective_id=0, has_side_effects=True, vmem_limit_bytes=67_043_328
        ),
    )(
        block_node,
        ghost_source,
        block_node.reshape(1, blocks),
        cost,
        flow_start,
        capacity.reshape(arc_blocks, BLK),
        cap_dual_start.reshape(arc_blocks, BLK),
        demand,
        node_dual_start,
        incidence,
    )
    return flow_end, cap_end.reshape(arcs), node_end


def solution(mesh):
    return jax.shard_map(
        body,
        mesh=mesh,
        in_specs=(
            P("comm", "region"),
            P("comm", "region"),
            P("region"),
            P("region"),
            P("comm", "region"),
            P("comm", "region"),
            P("region", None, None),
            P("region"),
            P("region"),
        ),
        out_specs=(P("comm", "region"), P("region"), P("comm", "region")),
        check_vma=False,
    )
```

```python
import functools

import jax
import jax.numpy as jnp
from jax import lax
from jax.experimental import pallas as pl
from jax.experimental.pallas import tpu as pltpu
from jax.sharding import PartitionSpec as P

BPA = 2
NBD = 4
NG = 8
ITERS = 2
BLK = 128
Z_SIZE = 8
CHUNKS = 8
UNROLL = 8
ROW_PAD = 64

step_scale = 0.08
MESH = pl.DeviceIdType.MESH


def split(value):
    high = value.astype(jnp.bfloat16)
    low = (value - high.astype(jnp.float32)).astype(jnp.bfloat16)
    return high, low


def columns(block):
    if isinstance(block, int):
        return pl.ds(block * BLK, BLK)
    return pl.ds(pl.multiple_of(block * BLK, BLK), BLK)


def square_sum(ref, width):
    def step(index, total):
        for part in range(4):
            piece = ref[:, columns(index * 4 + part)]
            squares = piece * piece
            total = total + (squares[:8] + squares[8:])
        return total

    return lax.fori_loop(0, width // (4 * BLK), step, jnp.zeros((8, BLK), jnp.float32))


def kernel(
    regions,
    comms,
    bn_hbm,
    gs_hbm,
    bn_row_hbm,
    cost_hbm,
    flow_hbm,
    capacity_hbm,
    cap_dual_hbm,
    demand_hbm,
    node_dual_hbm,
    inc_hbm,
    flow_o,
    cap_o,
    nd_o,
    bn,
    gs,
    bn_row,
    cost,
    flow,
    capacity,
    cap_dual,
    demand,
    node_dual,
    inc_buf,
    w2,
    back_s,
    nd3,
    dtab,
    oh2,
    cand,
    fwd,
    slot,
    rbuf,
    load_s,
    ld_a,
    ld_b,
    sbuf,
    arg_sem,
    inc_sem,
    sc_send,
    sc_recv,
    gh_send,
    gh_recv,
    rt_send,
    rt_recv,
    ld_send,
    ld_recv,
):
    r = lax.axis_index("region")
    c = lax.axis_index("comm")
    own = nd3.shape[0]
    arc_blocks = w2.shape[0]
    commodities = cost.shape[0]
    x_size = regions // Z_SIZE
    x = r // Z_SIZE
    z = lax.rem(r, Z_SIZE)
    deltas = (1, 2, regions - 2, regions - 1, regions // 2)
    per_chunk = inc_buf.shape[0] // CHUNKS
    load_rows = load_s.shape[0] // comms

    arg_copies = {}
    for index, (name, source, target) in enumerate(
        (
            ("cost", cost_hbm, cost),
            ("node_dual", node_dual_hbm, node_dual),
            ("demand", demand_hbm, demand),
            ("gs", gs_hbm, gs),
            ("bn_row", bn_row_hbm, bn_row),
            ("bn", bn_hbm, bn),
            ("capacity", capacity_hbm, capacity),
            ("cap_dual", cap_dual_hbm, cap_dual),
            ("flow", flow_hbm, flow),
        )
    ):
        copy = pltpu.make_async_copy(source, target, arg_sem.at[index])
        copy.start()
        arg_copies[name] = copy
    inc_copies = []
    for chunk in range(CHUNKS):
        rows = pl.ds(chunk * per_chunk, per_chunk)
        copy = pltpu.make_async_copy(inc_hbm.at[rows], inc_buf.at[rows], inc_sem.at[chunk])
        copy.start()
        inc_copies.append(copy)

    def comm_peer(off):
        return {"region": r, "comm": lax.rem(c + off, comms)}

    def x_peer(off):
        return {"region": lax.rem(x + off, x_size) * Z_SIZE + z, "comm": c}

    def z_peer(off):
        return {"region": x * Z_SIZE + lax.rem(z + off, Z_SIZE), "comm": c}

    def r_peer(off):
        return {"region": lax.rem(r + off, regions), "comm": c}

    barrier = pltpu.get_barrier_semaphore()
    greeted = 0
    for peer, offs in (
        (comm_peer, range(1, comms)),
        (x_peer, range(1, x_size)),
        (z_peer, range(1, Z_SIZE)),
        (r_peer, deltas[:4]),
    ):
        for off in offs:
            pl.semaphore_signal(barrier, inc=1, device_id=peer(off), device_id_type=MESH)
            greeted += 1

    def spread(index, carry):
        for part in range(4):
            s = index * 4 + part
            value = node_dual[:, columns(s)]
            nd3[s] = value
            high, low = split(value)
            dtab[s, 0:commodities] = high
            dtab[s, commodities:] = low
        return carry

    arg_copies["cost"].wait()
    sbuf[0, c, 0:8] = square_sum(cost, cost.shape[1])
    arg_copies["demand"].wait()
    sbuf[0, c, 8:16] = square_sum(demand, demand.shape[1])
    arg_copies["node_dual"].wait()
    lax.fori_loop(0, own // 4, spread, 0)
    for j in range(NBD):
        cand[j] = node_dual[:, columns(j)]

    pl.semaphore_wait(barrier, greeted)

    def send_scalars(stage, peer, count, me):
        copies = []
        for off in range(1, count):
            copy = pltpu.make_async_remote_copy(
                src_ref=sbuf.at[stage, me],
                dst_ref=sbuf.at[stage, me],
                send_sem=sc_send.at[stage, off],
                recv_sem=sc_recv.at[stage, off],
                device_id=peer(off),
                device_id_type=MESH,
            )
            copy.start()
            copies.append(copy)
        return copies

    def take_scalars(stage, copies):
        for copy in copies:
            copy.wait()
        total = sbuf[stage, 0]
        for index in range(1, len(copies) + 1):
            total = total + sbuf[stage, index]
        return total

    def send_ghosts(it):
        copies = []
        for index, delta in enumerate(deltas):
            copy = pltpu.make_async_remote_copy(
                src_ref=nd3.at[pl.ds(0, NBD)],
                dst_ref=cand.at[pl.ds(it * 24 + (index + 1) * NBD, NBD)],
                send_sem=gh_send.at[it, index],
                recv_sem=gh_recv.at[it, index],
                device_id=r_peer(regions - delta),
                device_id_type=MESH,
            )
            copy.start()
            copies.append(copy)
        return copies

    blocks_of = arc_blocks // CHUNKS

    def convert(chunk, first=0, end=blocks_of):
        if first == 0:
            inc_copies[chunk].wait()

        def step(index, carry):
            a = chunk * blocks_of + index
            for b in range(BPA):
                high, low = split(inc_buf[a * BPA + b])
                w2[a, b * BLK : (b + 1) * BLK, 0:BLK] = high
                w2[a, b * BLK : (b + 1) * BLK, BLK:] = low
            return carry

        lax.fori_loop(first, end, step, 0)

    scalar_copies = send_scalars(0, comm_peer, comms, c)
    ghost_copies = send_ghosts(0)
    arg_copies["gs"].wait()
    arg_copies["bn_row"].wait()
    ghost_at = []
    code = bn_row[...]
    slots = code
    for g in range(NG):
        source = gs[g]
        block = source & (NBD - 1)
        delta = lax.rem((source >> 2) - r + regions, regions)
        behind = jnp.maximum(delta - (regions - 5), 3)
        relation = jnp.where(delta <= 2, delta, jnp.where(delta == regions // 2, 5, behind))
        ghost_at.append(relation * NBD + block)
        row = jnp.where(relation == 0, block, own - NBD + relation * NBD + block)
        code = jnp.where(slots == own + g, row, code)
    hits = lax.broadcasted_iota(jnp.int32, (ROW_PAD, BLK), 0) == code
    one_hot = jnp.where(hits, 1.0, 0.0).astype(jnp.bfloat16)
    oh2[:, 0:BLK] = one_hot
    oh2[:, BLK:] = one_hot

    for chunk in range(0, 2):
        convert(chunk)
    arg_copies["capacity"].wait()
    cap_sq = jnp.zeros((8, BLK), jnp.float32)
    for part in range(capacity.shape[0] // 8):
        piece = capacity[part * 8 : (part + 1) * 8]
        cap_sq = cap_sq + piece * piece
    total = take_scalars(0, scalar_copies)
    sbuf[1, x, 0:8] = total[0:8]
    sbuf[1, x, 8:16] = total[8:16] + cap_sq
    convert(2, 0, 1)
    scalar_copies = send_scalars(1, x_peer, x_size, x)
    convert(2, 1)
    for chunk in range(3, 5):
        convert(chunk)
    total = take_scalars(1, scalar_copies)
    sbuf[2, z] = total
    convert(5, 0, 1)
    scalar_copies = send_scalars(2, z_peer, Z_SIZE, z)
    convert(5, 1)
    for chunk in range(6, 8):
        convert(chunk)

    arg_copies["bn"].wait()
    arg_copies["cap_dual"].wait()
    arg_copies["flow"].wait()

    primal_step = None
    dual_step = None
    for it in range(ITERS):
        last = it == ITERS - 1
        flow_src = flow if it == 0 else flow_o
        cap_src = cap_dual if it == 0 else cap_o

        for copy in ghost_copies:
            copy.wait()
        for g in range(NG):
            high, low = split(cand[it * 24 + ghost_at[g]])
            dtab[own + g, 0:commodities] = high
            dtab[own + g, commodities:] = low

        def back_of(a):
            left = dtab[bn[a * BPA]]
            right = dtab[bn[a * BPA + 1]]
            product = jnp.dot(
                jnp.concatenate([left, right], axis=1),
                w2[a],
                preferred_element_type=jnp.float32,
            )
            half = product[:commodities] + product[commodities:]
            return half[:, :BLK] + half[:, BLK:]

        def update(a, back):
            now = flow_src[:, columns(a)]
            price = cost[:, columns(a)] - back + cap_src[pl.ds(a, 1), :]
            new = jnp.maximum(now - primal_step * price, 0.0)
            bar = 2.0 * new - now
            flow_o[:, columns(a)] = new
            load_s[pl.ds(a, 1), :] = jnp.sum(bar, axis=0, keepdims=True)
            back_s[:, columns(a)] = bar

        def back_step(index, carry):
            for part in range(UNROLL):
                a = index * UNROLL + part
                back_s[:, columns(a)] = back_of(a)
            return carry

        def update_step(index, carry):
            for part in range(UNROLL):
                a = index * UNROLL + part
                update(a, back_s[:, columns(a)])
            return carry

        def both_step(index, carry):
            for part in range(UNROLL):
                a = index * UNROLL + part
                update(a, back_of(a))
            return carry

        if it == 0:
            lax.fori_loop(0, arc_blocks // UNROLL, back_step, 0)
            total = take_scalars(2, scalar_copies)
            cost_all = jnp.sum(total[0:8], axis=(0, 1), keepdims=True)
            rest_all = jnp.sum(total[8:16], axis=(0, 1), keepdims=True)
            weight = jnp.sqrt(cost_all / rest_all)
            primal_step = jnp.broadcast_to(step_scale / weight, (1, BLK))
            dual_step = jnp.broadcast_to(step_scale * weight, (1, BLK))
            lax.fori_loop(0, arc_blocks // UNROLL, update_step, 0)
        else:
            lax.fori_loop(0, arc_blocks // UNROLL, both_step, 0)

        load_copies = []
        for off in range(1, comms):
            target = lax.rem(c + off, comms)
            copy = pltpu.make_async_remote_copy(
                src_ref=load_s.at[
                    pl.ds(pl.multiple_of(target * load_rows, load_rows), load_rows)
                ],
                dst_ref=ld_a.at[it, c],
                send_sem=ld_send.at[it, 0, off],
                recv_sem=ld_recv.at[it, 0, off],
                device_id=comm_peer(off),
                device_id_type=MESH,
            )
            copy.start()
            load_copies.append(copy)

        def forward_step(index, carry):
            for part in range(UNROLL):
                a = index * UNROLL + part
                high, low = split(back_s[:, columns(a)])
                terms = jnp.concatenate(
                    [
                        jnp.concatenate([high, high], axis=1),
                        jnp.concatenate([low, low], axis=1),
                    ],
                    axis=0,
                )
                product = lax.dot_general(
                    terms,
                    w2[a],
                    (((1,), (1,)), ((), ())),
                    preferred_element_type=jnp.float32,
                )
                half = product[:commodities] + product[commodities:]
                row = pl.multiple_of(a * (BPA * commodities), BPA * commodities)
                fwd[pl.ds(row, commodities), :] = half[:, :BLK]
                fwd[pl.ds(row + commodities, commodities), :] = half[:, BLK:]
            return carry

        lax.fori_loop(0, arc_blocks // UNROLL, forward_step, 0)

        blocks = BPA * arc_blocks
        for pair in range(commodities // 2):
            high_0, low_0 = split(fwd[pl.ds(2 * pair, blocks, stride=commodities), :])
            high_1, low_1 = split(fwd[pl.ds(2 * pair + 1, blocks, stride=commodities), :])
            terms = jnp.concatenate(
                [
                    jnp.concatenate([high_0, high_1], axis=1),
                    jnp.concatenate([low_0, low_1], axis=1),
                ],
                axis=0,
            )
            rows = jnp.dot(oh2[...], terms, preferred_element_type=jnp.float32)
            slot[pl.ds(2 * pair, ROW_PAD, stride=commodities), :] = rows[:, :BLK]
            slot[pl.ds(2 * pair + 1, ROW_PAD, stride=commodities), :] = rows[:, BLK:]

        def updated(s, rows):
            return nd3[s] + dual_step * (demand[:, columns(s)] - rows)

        def keep(s, value):
            if last:
                nd_o[:, columns(s)] = value
            else:
                nd3[s] = value
                high, low = split(value)
                dtab[s, 0:commodities] = high
                dtab[s, commodities:] = low

        def inner_step(index, carry):
            for part in range(4):
                s = NBD + index * 4 + part
                row = pl.multiple_of(s * commodities, commodities)
                keep(s, updated(s, slot[pl.ds(row, commodities), :]))
            return carry

        lax.fori_loop(0, 1, inner_step, 0)

        routed_copies = []
        for index, delta in enumerate(deltas):
            rows = NBD * commodities
            copy = pltpu.make_async_remote_copy(
                src_ref=slot.at[pl.ds(own * commodities + index * rows, rows)],
                dst_ref=rbuf.at[it, index],
                send_sem=rt_send.at[it, index],
                recv_sem=rt_recv.at[it, index],
                device_id=r_peer(delta),
                device_id_type=MESH,
            )
            copy.start()
            routed_copies.append(copy)

        for copy in load_copies:
            copy.wait()
        mine = load_s[pl.ds(pl.multiple_of(c * load_rows, load_rows), load_rows), :]
        for off in range(1, comms):
            mine = mine + ld_a[it, lax.rem(c + off, comms)]
        ld_b[it, c] = mine

        lax.fori_loop(1, (own - NBD) // 4, inner_step, 0)

        total_copies = []
        for off in range(1, comms):
            copy = pltpu.make_async_remote_copy(
                src_ref=ld_b.at[it, c],
                dst_ref=ld_b.at[it, c],
                send_sem=ld_send.at[it, 1, off],
                recv_sem=ld_recv.at[it, 1, off],
                device_id=comm_peer(off),
                device_id_type=MESH,
            )
            copy.start()
            total_copies.append(copy)

        def finish_load(at, copies=total_copies, source=cap_src):
            for copy in copies:
                copy.wait()
            for owner in range(comms):
                rows = slice(owner * load_rows, (owner + 1) * load_rows)
                excess = ld_b[at, owner] - capacity[rows]
                cap_o[rows] = jnp.maximum(source[rows] + dual_step * excess, 0.0)

        for copy in routed_copies:
            copy.wait()
        for j in range(NBD):
            rows = slot[j * commodities : (j + 1) * commodities, :]
            for index in range(len(deltas)):
                rows = rows + rbuf[it, index, j * commodities : (j + 1) * commodities, :]
            value = updated(j, rows)
            keep(j, value)
            if not last:
                cand[(it + 1) * 24 + j] = value
        if last:
            finish_load(it)
        else:
            ghost_copies = send_ghosts(it + 1)
            finish_load(it)


def settle(count, *refs):
    sources, targets, sem = refs[:count], refs[count : 2 * count], refs[2 * count]
    leaving = []
    for index in range(count):
        rows = sources[index].shape[0] // 2
        for part in range(2):
            at = pl.ds(part * rows, rows)
            copy = pltpu.make_async_copy(
                sources[index].at[at], targets[index].at[at], sem.at[index, part]
            )
            copy.start()
            leaving.append(copy)
    for copy in leaving:
        copy.wait()


def body(
    cost,
    flow_start,
    capacity,
    cap_dual_start,
    demand,
    node_dual_start,
    incidence,
    block_node,
    ghost_source,
):
    regions = lax.axis_size("region")
    comms = lax.axis_size("comm")
    commodities, arcs = cost.shape
    nodes = demand.shape[1]
    arc_blocks = arcs // BLK
    own = nodes // BLK
    blocks = incidence.shape[0]
    f32, bf16 = jnp.float32, jnp.bfloat16
    hbm = pl.BlockSpec(memory_space=pltpu.HBM)
    vmem = pl.BlockSpec(memory_space=pltpu.VMEM)
    dma = pltpu.SemaphoreType.DMA
    relations = 5
    flow_end, cap_end, node_end = pl.pallas_call(
        functools.partial(kernel, regions, comms),
        name="pdhg",
        out_shape=(
            jax.ShapeDtypeStruct((commodities, arcs), f32),
            jax.ShapeDtypeStruct((arc_blocks, BLK), f32),
            jax.ShapeDtypeStruct((commodities, nodes), f32),
        ),
        in_specs=[hbm] * 10,
        out_specs=(vmem, vmem, vmem),
        scratch_shapes=[
            pltpu.SMEM((blocks,), jnp.int32),
            pltpu.SMEM((NG,), jnp.int32),
            pltpu.VMEM((1, blocks), jnp.int32),
            pltpu.VMEM((commodities, arcs), f32),
            pltpu.VMEM((commodities, arcs), f32),
            pltpu.VMEM((arc_blocks, BLK), f32),
            pltpu.VMEM((arc_blocks, BLK), f32),
            pltpu.VMEM((commodities, nodes), f32),
            pltpu.VMEM((commodities, nodes), f32),
            pltpu.VMEM((blocks, BLK, BLK), f32),
            pltpu.VMEM((arc_blocks, BPA * BLK, 2 * BLK), bf16),
            pltpu.VMEM((commodities, arcs), f32),
            pltpu.VMEM((own, commodities, BLK), f32),
            pltpu.VMEM((own + NG, 2 * commodities, BLK), bf16),
            pltpu.VMEM((ROW_PAD, 2 * BLK), bf16),
            pltpu.VMEM((ITERS * 24, commodities, BLK), f32),
            pltpu.VMEM((blocks * commodities, BLK), f32),
            pltpu.VMEM((ROW_PAD * commodities, BLK), f32),
            pltpu.VMEM((ITERS, relations, NBD * commodities, BLK), f32),
            pltpu.VMEM((arc_blocks, BLK), f32),
            pltpu.VMEM((ITERS, comms, arc_blocks // comms, BLK), f32),
            pltpu.VMEM((ITERS, comms, arc_blocks // comms, BLK), f32),
            pltpu.VMEM((3, 8, 16, BLK), f32),
            dma((9,)),
            dma((CHUNKS,)),
            dma((3, 8)),
            dma((3, 8)),
            dma((ITERS, relations)),
            dma((ITERS, relations)),
            dma((ITERS, relations)),
            dma((ITERS, relations)),
            dma((ITERS, 2, 8)),
            dma((ITERS, 2, 8)),
        ],
        compiler_params=pltpu.CompilerParams(
            collective_id=0, has_side_effects=True, vmem_limit_bytes=50_000_000
        ),
    )(
        *(
            pltpu.with_memory_space_constraint(value, pltpu.HBM)
            for value in (
                block_node,
                ghost_source,
                block_node.reshape(1, blocks),
                cost,
                flow_start,
                capacity.reshape(arc_blocks, BLK),
                cap_dual_start.reshape(arc_blocks, BLK),
                demand,
                node_dual_start,
                incidence,
            )
        )
    )
    shapes = (flow_end.shape, cap_end.shape, node_end.shape)
    flow_end, cap_end, node_end = pl.pallas_call(
        functools.partial(settle, 3),
        name="settle",
        out_shape=tuple(jax.ShapeDtypeStruct(shape, f32) for shape in shapes),
        in_specs=[vmem] * 3,
        out_specs=(hbm, hbm, hbm),
        scratch_shapes=[dma((3, 2))],
        compiler_params=pltpu.CompilerParams(vmem_limit_bytes=1024 * 1024),
    )(flow_end, cap_end, node_end)
    return flow_end, cap_end.reshape(arcs), node_end


def solution(mesh):
    return jax.shard_map(
        body,
        mesh=mesh,
        in_specs=(
            P("comm", "region"),
            P("comm", "region"),
            P("region"),
            P("region"),
            P("comm", "region"),
            P("comm", "region"),
            P("region", None, None),
            P("region"),
            P("region"),
        ),
        out_specs=(P("comm", "region"), P("region"), P("comm", "region")),
        check_vma=False,
    )
```

```python
import functools

import jax
import jax.numpy as jnp
from jax import lax
from jax.experimental import pallas as pl
from jax.experimental.pallas import tpu as pltpu
from jax.sharding import PartitionSpec as P

BPA = 2
NBD = 4
NG = 8
ITERS = 2
BLK = 128
Z_SIZE = 8
CHUNKS = 8
UNROLL = 8
ROW_PAD = 64

step_scale = 0.08
MESH = pl.DeviceIdType.MESH


def split(value):
    high = value.astype(jnp.bfloat16)
    low = (value - high.astype(jnp.float32)).astype(jnp.bfloat16)
    return high, low


def columns(block):
    if isinstance(block, int):
        return pl.ds(block * BLK, BLK)
    return pl.ds(pl.multiple_of(block * BLK, BLK), BLK)


def square_sum(ref, width):
    def step(index, total):
        for part in range(4):
            piece = ref[:, columns(index * 4 + part)]
            squares = piece * piece
            total = total + (squares[:8] + squares[8:])
        return total

    return lax.fori_loop(0, width // (4 * BLK), step, jnp.zeros((8, BLK), jnp.float32))


def kernel(
    regions,
    comms,
    bn_hbm,
    gs_hbm,
    bn_row_hbm,
    cost_hbm,
    flow_hbm,
    capacity_hbm,
    cap_dual_hbm,
    demand_hbm,
    node_dual_hbm,
    inc_hbm,
    flow_o,
    cap_o,
    nd_o,
    bn,
    gs,
    bn_row,
    cost,
    flow,
    capacity,
    cap_dual,
    demand,
    node_dual,
    inc_buf,
    w2,
    back_s,
    nd3,
    dtab,
    oh2,
    cand,
    fwd,
    slot,
    rbuf,
    load_s,
    ld_a,
    ld_b,
    sbuf,
    pick_out,
    pick_in,
    far_out,
    pick_send,
    pick_recv,
    arg_sem,
    inc_sem,
    sc_send,
    sc_recv,
    gh_send,
    gh_recv,
    rt_send,
    rt_recv,
    ld_send,
    ld_recv,
):
    r = lax.axis_index("region")
    c = lax.axis_index("comm")
    own = nd3.shape[0]
    arc_blocks = w2.shape[0]
    commodities = cost.shape[0]
    x_size = regions // Z_SIZE
    x = r // Z_SIZE
    z = lax.rem(r, Z_SIZE)
    order = (4, 1, 2, 0, 3)
    deltas = (1, 2, regions - 2, regions - 1, regions // 2)
    per_chunk = inc_buf.shape[0] // CHUNKS
    load_rows = load_s.shape[0] // comms

    arg_copies = {}
    for index, (name, source, target) in enumerate(
        (
            ("cost", cost_hbm, cost),
            ("node_dual", node_dual_hbm, node_dual),
            ("demand", demand_hbm, demand),
            ("gs", gs_hbm, gs),
            ("bn_row", bn_row_hbm, bn_row),
            ("bn", bn_hbm, bn),
            ("capacity", capacity_hbm, capacity),
            ("cap_dual", cap_dual_hbm, cap_dual),
            ("flow", flow_hbm, flow),
        )
    ):
        copy = pltpu.make_async_copy(source, target, arg_sem.at[index])
        copy.start()
        arg_copies[name] = copy
    inc_copies = []
    for chunk in range(CHUNKS):
        rows = pl.ds(chunk * per_chunk, per_chunk)
        copy = pltpu.make_async_copy(inc_hbm.at[rows], inc_buf.at[rows], inc_sem.at[chunk])
        copy.start()
        inc_copies.append(copy)

    def comm_peer(off):
        return {"region": r, "comm": lax.rem(c + off, comms)}

    def x_peer(off):
        return {"region": lax.rem(x + off, x_size) * Z_SIZE + z, "comm": c}

    def z_peer(off):
        return {"region": x * Z_SIZE + lax.rem(z + off, Z_SIZE), "comm": c}

    def r_peer(off):
        return {"region": lax.rem(r + off, regions), "comm": c}

    barrier = pltpu.get_barrier_semaphore()
    greeted = 0
    for peer, offs in (
        (comm_peer, range(1, comms)),
        (x_peer, range(1, x_size)),
        (z_peer, range(1, Z_SIZE)),
        (r_peer, deltas[:4]),
    ):
        for off in offs:
            pl.semaphore_signal(barrier, inc=1, device_id=peer(off), device_id_type=MESH)
            greeted += 1

    def spread(index, carry):
        for part in range(4):
            s = index * 4 + part
            value = node_dual[:, columns(s)]
            nd3[s] = value
            high, low = split(value)
            dtab[s, 0:commodities] = high
            dtab[s, commodities:] = low
        return carry

    arg_copies["cost"].wait()
    sbuf[0, c, 0:8] = square_sum(cost, cost.shape[1])
    arg_copies["demand"].wait()
    sbuf[0, c, 8:16] = square_sum(demand, demand.shape[1])
    arg_copies["node_dual"].wait()
    lax.fori_loop(0, own // 4, spread, 0)
    for j in range(NBD):
        cand[j] = node_dual[:, columns(j)]

    pl.semaphore_wait(barrier, greeted)

    def send_scalars(stage, peer, count, me):
        copies = []
        for off in range(1, count):
            copy = pltpu.make_async_remote_copy(
                src_ref=sbuf.at[stage, me],
                dst_ref=sbuf.at[stage, me],
                send_sem=sc_send.at[stage, off],
                recv_sem=sc_recv.at[stage, off],
                device_id=peer(off),
                device_id_type=MESH,
            )
            copy.start()
            copies.append(copy)
        return copies

    def take_scalars(stage, copies):
        for copy in copies:
            copy.wait()
        total = sbuf[stage, 0]
        for index in range(1, len(copies) + 1):
            total = total + sbuf[stage, index]
        return total

    def send_ghosts(it):
        copies = []
        for index in order:
            delta = deltas[index]
            far = index == 4 and it > 0
            count = 1 if far else NBD
            copy = pltpu.make_async_remote_copy(
                src_ref=far_out if far else nd3.at[pl.ds(0, NBD)],
                dst_ref=cand.at[pl.ds(it * 24 + (index + 1) * NBD, count)],
                send_sem=gh_send.at[it, index],
                recv_sem=gh_recv.at[it, index],
                device_id=r_peer(regions - delta),
                device_id_type=MESH,
            )
            copy.start()
            copies.append(copy)
        return copies

    blocks_of = arc_blocks // CHUNKS

    def convert(chunk, first=0, end=blocks_of):
        if first == 0:
            inc_copies[chunk].wait()

        def step(index, carry):
            a = chunk * blocks_of + index
            for b in range(BPA):
                high, low = split(inc_buf[a * BPA + b])
                w2[a, b * BLK : (b + 1) * BLK, 0:BLK] = high
                w2[a, b * BLK : (b + 1) * BLK, BLK:] = low
            return carry

        lax.fori_loop(first, end, step, 0)

    scalar_copies = send_scalars(0, comm_peer, comms, c)
    ghost_copies = send_ghosts(0)
    arg_copies["gs"].wait()
    arg_copies["bn_row"].wait()
    ghost_at = []
    ghost_later = []
    code = bn_row[...]
    slots = code
    for g in range(NG):
        source = gs[g]
        block = source & (NBD - 1)
        delta = lax.rem((source >> 2) - r + regions, regions)
        behind = jnp.maximum(delta - (regions - 5), 3)
        relation = jnp.where(delta <= 2, delta, jnp.where(delta == regions // 2, 5, behind))
        ghost_at.append(relation * NBD + block)
        ghost_later.append(jnp.where(relation == 5, 5 * NBD, relation * NBD + block))
        row = jnp.where(
            relation == 0, block, jnp.where(relation == 5, own, own + block) + (relation - 1) * NBD
        )
        code = jnp.where(slots == own + g, row, code)
    hits = lax.broadcasted_iota(jnp.int32, (ROW_PAD, BLK), 0) == code
    one_hot = jnp.where(hits, 1.0, 0.0).astype(jnp.bfloat16)
    oh2[:, 0:BLK] = one_hot
    oh2[:, BLK:] = one_hot

    far_block = gs[0] & (NBD - 1)
    pick_out[...] = jnp.full(pick_out.shape, far_block, jnp.int32).astype(jnp.float32)

    for chunk in range(0, 2):
        convert(chunk)
    arg_copies["capacity"].wait()
    cap_sq = jnp.zeros((8, BLK), jnp.float32)
    for part in range(capacity.shape[0] // 8):
        piece = capacity[part * 8 : (part + 1) * 8]
        cap_sq = cap_sq + piece * piece
    pick_copy = pltpu.make_async_remote_copy(
        src_ref=pick_out,
        dst_ref=pick_in,
        send_sem=pick_send.at[0],
        recv_sem=pick_recv.at[0],
        device_id=r_peer(regions // 2),
        device_id_type=MESH,
    )
    pick_copy.start()
    total = take_scalars(0, scalar_copies)
    sbuf[1, x, 0:8] = total[0:8]
    sbuf[1, x, 8:16] = total[8:16] + cap_sq
    convert(2, 0, 1)
    scalar_copies = send_scalars(1, x_peer, x_size, x)
    convert(2, 1)
    for chunk in range(3, 5):
        convert(chunk)
    total = take_scalars(1, scalar_copies)
    sbuf[2, z] = total
    convert(5, 0, 1)
    scalar_copies = send_scalars(2, z_peer, Z_SIZE, z)
    convert(5, 1)
    for chunk in range(6, 8):
        convert(chunk)

    arg_copies["bn"].wait()
    arg_copies["cap_dual"].wait()
    arg_copies["flow"].wait()

    primal_step = None
    dual_step = None
    for it in range(ITERS):
        last = it == ITERS - 1
        flow_src = flow if it == 0 else flow_o
        cap_src = cap_dual if it == 0 else cap_o

        for copy in ghost_copies:
            copy.wait()
        for g in range(NG):
            high, low = split(cand[it * 24 + (ghost_later if it else ghost_at)[g]])
            dtab[own + g, 0:commodities] = high
            dtab[own + g, commodities:] = low

        def back_of(a):
            left = dtab[bn[a * BPA]]
            right = dtab[bn[a * BPA + 1]]
            product = jnp.dot(
                jnp.concatenate([left, right], axis=1),
                w2[a],
                preferred_element_type=jnp.float32,
            )
            half = product[:commodities] + product[commodities:]
            return half[:, :BLK] + half[:, BLK:]

        def update(a, back):
            now = flow_src[:, columns(a)]
            price = cost[:, columns(a)] - back + cap_src[pl.ds(a, 1), :]
            new = jnp.maximum(now - primal_step * price, 0.0)
            bar = 2.0 * new - now
            flow_o[:, columns(a)] = new
            load_s[pl.ds(a, 1), :] = jnp.sum(bar, axis=0, keepdims=True)
            back_s[:, columns(a)] = bar

        def back_step(index, carry):
            for part in range(UNROLL):
                a = index * UNROLL + part
                back_s[:, columns(a)] = back_of(a)
            return carry

        def update_step(index, carry):
            for part in range(UNROLL):
                a = index * UNROLL + part
                update(a, back_s[:, columns(a)])
            return carry

        def both_step(index, carry):
            for part in range(UNROLL):
                a = index * UNROLL + part
                update(a, back_of(a))
            return carry

        if it == 0:
            lax.fori_loop(0, arc_blocks // UNROLL, back_step, 0)
            total = take_scalars(2, scalar_copies)
            cost_all = jnp.sum(total[0:8], axis=(0, 1), keepdims=True)
            rest_all = jnp.sum(total[8:16], axis=(0, 1), keepdims=True)
            weight = jnp.sqrt(cost_all / rest_all)
            primal_step = jnp.broadcast_to(step_scale / weight, (1, BLK))
            dual_step = jnp.broadcast_to(step_scale * weight, (1, BLK))
            lax.fori_loop(0, arc_blocks // UNROLL, update_step, 0)
        else:
            lax.fori_loop(0, arc_blocks // UNROLL, both_step, 0)

        load_copies = []
        for off in range(1, comms):
            target = lax.rem(c + off, comms)
            copy = pltpu.make_async_remote_copy(
                src_ref=load_s.at[
                    pl.ds(pl.multiple_of(target * load_rows, load_rows), load_rows)
                ],
                dst_ref=ld_a.at[it, c],
                send_sem=ld_send.at[it, 0, off],
                recv_sem=ld_recv.at[it, 0, off],
                device_id=comm_peer(off),
                device_id_type=MESH,
            )
            copy.start()
            load_copies.append(copy)

        def forward_step(index, carry):
            for part in range(UNROLL):
                a = index * UNROLL + part
                high, low = split(back_s[:, columns(a)])
                terms = jnp.concatenate(
                    [
                        jnp.concatenate([high, high], axis=1),
                        jnp.concatenate([low, low], axis=1),
                    ],
                    axis=0,
                )
                product = lax.dot_general(
                    terms,
                    w2[a],
                    (((1,), (1,)), ((), ())),
                    preferred_element_type=jnp.float32,
                )
                half = product[:commodities] + product[commodities:]
                row = pl.multiple_of(a * (BPA * commodities), BPA * commodities)
                fwd[pl.ds(row, commodities), :] = half[:, :BLK]
                fwd[pl.ds(row + commodities, commodities), :] = half[:, BLK:]
            return carry

        lax.fori_loop(0, arc_blocks // UNROLL, forward_step, 0)

        blocks = BPA * arc_blocks
        for pair in range(commodities // 2):
            high_0, low_0 = split(fwd[pl.ds(2 * pair, blocks, stride=commodities), :])
            high_1, low_1 = split(fwd[pl.ds(2 * pair + 1, blocks, stride=commodities), :])
            terms = jnp.concatenate(
                [
                    jnp.concatenate([high_0, high_1], axis=1),
                    jnp.concatenate([low_0, low_1], axis=1),
                ],
                axis=0,
            )
            rows = jnp.dot(oh2[...], terms, preferred_element_type=jnp.float32)
            slot[pl.ds(2 * pair, ROW_PAD, stride=commodities), :] = rows[:, :BLK]
            slot[pl.ds(2 * pair + 1, ROW_PAD, stride=commodities), :] = rows[:, BLK:]

        def updated(s, rows):
            return nd3[s] + dual_step * (demand[:, columns(s)] - rows)

        def keep(s, value):
            if last:
                nd_o[:, columns(s)] = value
            else:
                nd3[s] = value
                high, low = split(value)
                dtab[s, 0:commodities] = high
                dtab[s, commodities:] = low

        def inner_step(index, carry):
            for part in range(4):
                s = NBD + index * 4 + part
                row = pl.multiple_of(s * commodities, commodities)
                keep(s, updated(s, slot[pl.ds(row, commodities), :]))
            return carry

        lax.fori_loop(0, 1, inner_step, 0)

        routed_copies = []
        for index in order:
            delta = deltas[index]
            rows = NBD * commodities
            count = commodities if index == 4 else rows
            copy = pltpu.make_async_remote_copy(
                src_ref=slot.at[pl.ds(own * commodities + index * rows, count)],
                dst_ref=rbuf.at[it, index, pl.ds(0, count)],
                send_sem=rt_send.at[it, index],
                recv_sem=rt_recv.at[it, index],
                device_id=r_peer(delta),
                device_id_type=MESH,
            )
            copy.start()
            routed_copies.append(copy)

        for copy in load_copies:
            copy.wait()
        mine = load_s[pl.ds(pl.multiple_of(c * load_rows, load_rows), load_rows), :]
        for off in range(1, comms):
            mine = mine + ld_a[it, lax.rem(c + off, comms)]
        ld_b[it, c] = mine

        lax.fori_loop(1, (own - NBD) // 4, inner_step, 0)

        total_copies = []
        for off in range(1, comms):
            copy = pltpu.make_async_remote_copy(
                src_ref=ld_b.at[it, c],
                dst_ref=ld_b.at[it, c],
                send_sem=ld_send.at[it, 1, off],
                recv_sem=ld_recv.at[it, 1, off],
                device_id=comm_peer(off),
                device_id_type=MESH,
            )
            copy.start()
            total_copies.append(copy)

        def finish_load(at, copies=total_copies, source=cap_src):
            for copy in copies:
                copy.wait()
            for owner in range(comms):
                rows = slice(owner * load_rows, (owner + 1) * load_rows)
                excess = ld_b[at, owner] - capacity[rows]
                cap_o[rows] = jnp.maximum(source[rows] + dual_step * excess, 0.0)

        if it == 0:
            pick_copy.wait()
        picked = pick_in[...]
        for copy in routed_copies:
            copy.wait()
        far_value = jnp.zeros((commodities, BLK), jnp.float32)
        for j in range(NBD):
            rows = slot[j * commodities : (j + 1) * commodities, :]
            for index in range(4):
                rows = rows + rbuf[it, index, j * commodities : (j + 1) * commodities, :]
            rows = rows + jnp.where(picked == float(j), rbuf[it, 4, 0:commodities, :], 0.0)
            value = updated(j, rows)
            keep(j, value)
            if not last:
                cand[(it + 1) * 24 + j] = value
                far_value = jnp.where(picked == float(j), value, far_value)
        if not last:
            far_out[0] = far_value
        if last:
            finish_load(it)
        else:
            ghost_copies = send_ghosts(it + 1)
            finish_load(it)


def settle(count, *refs):
    sources, targets, sem = refs[:count], refs[count : 2 * count], refs[2 * count]
    leaving = []
    for index in range(count):
        rows = sources[index].shape[0] // 2
        for part in range(2):
            at = pl.ds(part * rows, rows)
            copy = pltpu.make_async_copy(
                sources[index].at[at], targets[index].at[at], sem.at[index, part]
            )
            copy.start()
            leaving.append(copy)
    for copy in leaving:
        copy.wait()


def body(
    cost,
    flow_start,
    capacity,
    cap_dual_start,
    demand,
    node_dual_start,
    incidence,
    block_node,
    ghost_source,
):
    regions = lax.axis_size("region")
    comms = lax.axis_size("comm")
    commodities, arcs = cost.shape
    nodes = demand.shape[1]
    arc_blocks = arcs // BLK
    own = nodes // BLK
    blocks = incidence.shape[0]
    f32, bf16 = jnp.float32, jnp.bfloat16
    hbm = pl.BlockSpec(memory_space=pltpu.HBM)
    vmem = pl.BlockSpec(memory_space=pltpu.VMEM)
    dma = pltpu.SemaphoreType.DMA
    relations = 5
    flow_end, cap_end, node_end = pl.pallas_call(
        functools.partial(kernel, regions, comms),
        name="pdhg",
        out_shape=(
            jax.ShapeDtypeStruct((commodities, arcs), f32),
            jax.ShapeDtypeStruct((arc_blocks, BLK), f32),
            jax.ShapeDtypeStruct((commodities, nodes), f32),
        ),
        in_specs=[hbm] * 10,
        out_specs=(vmem, vmem, vmem),
        scratch_shapes=[
            pltpu.SMEM((blocks,), jnp.int32),
            pltpu.SMEM((NG,), jnp.int32),
            pltpu.VMEM((1, blocks), jnp.int32),
            pltpu.VMEM((commodities, arcs), f32),
            pltpu.VMEM((commodities, arcs), f32),
            pltpu.VMEM((arc_blocks, BLK), f32),
            pltpu.VMEM((arc_blocks, BLK), f32),
            pltpu.VMEM((commodities, nodes), f32),
            pltpu.VMEM((commodities, nodes), f32),
            pltpu.VMEM((blocks, BLK, BLK), f32),
            pltpu.VMEM((arc_blocks, BPA * BLK, 2 * BLK), bf16),
            pltpu.VMEM((commodities, arcs), f32),
            pltpu.VMEM((own, commodities, BLK), f32),
            pltpu.VMEM((own + NG, 2 * commodities, BLK), bf16),
            pltpu.VMEM((ROW_PAD, 2 * BLK), bf16),
            pltpu.VMEM((ITERS * 24, commodities, BLK), f32),
            pltpu.VMEM((blocks * commodities, BLK), f32),
            pltpu.VMEM((ROW_PAD * commodities, BLK), f32),
            pltpu.VMEM((ITERS, relations, NBD * commodities, BLK), f32),
            pltpu.VMEM((arc_blocks, BLK), f32),
            pltpu.VMEM((ITERS, comms, arc_blocks // comms, BLK), f32),
            pltpu.VMEM((ITERS, comms, arc_blocks // comms, BLK), f32),
            pltpu.VMEM((3, 8, 16, BLK), f32),
            pltpu.VMEM((commodities, BLK), f32),
            pltpu.VMEM((commodities, BLK), f32),
            pltpu.VMEM((1, commodities, BLK), f32),
            dma((1,)),
            dma((1,)),
            dma((9,)),
            dma((CHUNKS,)),
            dma((3, 8)),
            dma((3, 8)),
            dma((ITERS, relations)),
            dma((ITERS, relations)),
            dma((ITERS, relations)),
            dma((ITERS, relations)),
            dma((ITERS, 2, 8)),
            dma((ITERS, 2, 8)),
        ],
        compiler_params=pltpu.CompilerParams(
            collective_id=0, has_side_effects=True, vmem_limit_bytes=50_000_000
        ),
    )(
        *(
            pltpu.with_memory_space_constraint(value, pltpu.HBM)
            for value in (
                block_node,
                ghost_source,
                block_node.reshape(1, blocks),
                cost,
                flow_start,
                capacity.reshape(arc_blocks, BLK),
                cap_dual_start.reshape(arc_blocks, BLK),
                demand,
                node_dual_start,
                incidence,
            )
        )
    )
    shapes = (flow_end.shape, cap_end.shape, node_end.shape)
    flow_end, cap_end, node_end = pl.pallas_call(
        functools.partial(settle, 3),
        name="settle",
        out_shape=tuple(jax.ShapeDtypeStruct(shape, f32) for shape in shapes),
        in_specs=[vmem] * 3,
        out_specs=(hbm, hbm, hbm),
        scratch_shapes=[dma((3, 2))],
        compiler_params=pltpu.CompilerParams(vmem_limit_bytes=1024 * 1024),
    )(flow_end, cap_end, node_end)
    return flow_end, cap_end.reshape(arcs), node_end


def solution(mesh):
    return jax.shard_map(
        body,
        mesh=mesh,
        in_specs=(
            P("comm", "region"),
            P("comm", "region"),
            P("region"),
            P("region"),
            P("comm", "region"),
            P("comm", "region"),
            P("region", None, None),
            P("region"),
            P("region"),
        ),
        out_specs=(P("comm", "region"), P("region"), P("comm", "region")),
        check_vma=False,
    )
```

```python
import functools

import jax
import jax.numpy as jnp
from jax import lax
from jax.experimental import pallas as pl
from jax.experimental.pallas import tpu as pltpu
from jax.sharding import PartitionSpec as P

BPA = 2
NBD = 4
NG = 8
ITERS = 2
BLK = 128
Z_SIZE = 8
CHUNKS = 8
UNROLL = 32
ROW_PAD = 64

step_scale = 0.08
MESH = pl.DeviceIdType.MESH


def split(value):
    high = value.astype(jnp.bfloat16)
    low = (value - high.astype(jnp.float32)).astype(jnp.bfloat16)
    return high, low


def columns(block):
    if isinstance(block, int):
        return pl.ds(block * BLK, BLK)
    return pl.ds(pl.multiple_of(block * BLK, BLK), BLK)


def square_sum(ref, width):
    def step(index, total):
        for part in range(4):
            piece = ref[:, columns(index * 4 + part)]
            squares = piece * piece
            total = total + (squares[:8] + squares[8:])
        return total

    return lax.fori_loop(0, width // (4 * BLK), step, jnp.zeros((8, BLK), jnp.float32))


def kernel(
    regions,
    comms,
    bn_hbm,
    gs_hbm,
    bn_row_hbm,
    cost_hbm,
    flow_hbm,
    capacity_hbm,
    cap_dual_hbm,
    demand_hbm,
    node_dual_hbm,
    inc_hbm,
    flow_o,
    cap_o,
    nd_o,
    bn,
    gs,
    bn_row,
    cost,
    flow,
    capacity,
    cap_dual,
    demand,
    node_dual,
    inc_buf,
    w2,
    back_s,
    nd3,
    dtab,
    oh2,
    cand,
    fwd,
    slot,
    rbuf,
    load_s,
    ld_a,
    ld_b,
    sbuf,
    pick_out,
    pick_in,
    far_out,
    pick_send,
    pick_recv,
    arg_sem,
    inc_sem,
    sc_send,
    sc_recv,
    gh_send,
    gh_recv,
    rt_send,
    rt_recv,
    ld_send,
    ld_recv,
):
    r = lax.axis_index("region")
    c = lax.axis_index("comm")
    own = nd3.shape[0]
    arc_blocks = w2.shape[0]
    commodities = cost.shape[0]
    x_size = regions // Z_SIZE
    x = r // Z_SIZE
    z = lax.rem(r, Z_SIZE)
    order = (4, 1, 2, 0, 3)
    deltas = (1, 2, regions - 2, regions - 1, regions // 2)
    per_chunk = inc_buf.shape[0] // CHUNKS
    load_rows = load_s.shape[0] // comms

    arg_copies = {}
    for index, (name, source, target) in enumerate(
        (
            ("cost", cost_hbm, cost),
            ("node_dual", node_dual_hbm, node_dual),
            ("demand", demand_hbm, demand),
            ("gs", gs_hbm, gs),
            ("bn_row", bn_row_hbm, bn_row),
            ("bn", bn_hbm, bn),
            ("capacity", capacity_hbm, capacity),
            ("cap_dual", cap_dual_hbm, cap_dual),
            ("flow", flow_hbm, flow),
        )
    ):
        copy = pltpu.make_async_copy(source, target, arg_sem.at[index])
        copy.start()
        arg_copies[name] = copy
    inc_copies = []
    for chunk in range(CHUNKS):
        rows = pl.ds(chunk * per_chunk, per_chunk)
        copy = pltpu.make_async_copy(inc_hbm.at[rows], inc_buf.at[rows], inc_sem.at[chunk])
        copy.start()
        inc_copies.append(copy)

    def comm_peer(off):
        return {"region": r, "comm": lax.rem(c + off, comms)}

    def x_peer(off):
        return {"region": lax.rem(x + off, x_size) * Z_SIZE + z, "comm": c}

    def z_peer(off):
        return {"region": x * Z_SIZE + lax.rem(z + off, Z_SIZE), "comm": c}

    def r_peer(off):
        return {"region": lax.rem(r + off, regions), "comm": c}

    barrier = pltpu.get_barrier_semaphore()
    greeted = 0
    for peer, offs in (
        (comm_peer, range(1, comms)),
        (x_peer, range(1, x_size)),
        (z_peer, range(1, Z_SIZE)),
        (r_peer, deltas[:4]),
    ):
        for off in offs:
            pl.semaphore_signal(barrier, inc=1, device_id=peer(off), device_id_type=MESH)
            greeted += 1

    def spread(index, carry):
        for part in range(4):
            s = index * 4 + part
            value = node_dual[:, columns(s)]
            nd3[s] = value
            high, low = split(value)
            dtab[s, 0:commodities] = high
            dtab[s, commodities:] = low
        return carry

    arg_copies["cost"].wait()
    sbuf[0, c, 0:8] = square_sum(cost, cost.shape[1])
    arg_copies["demand"].wait()
    sbuf[0, c, 8:16] = square_sum(demand, demand.shape[1])
    arg_copies["node_dual"].wait()
    lax.fori_loop(0, own // 4, spread, 0)
    for j in range(NBD):
        cand[j] = node_dual[:, columns(j)]

    pl.semaphore_wait(barrier, greeted)

    def send_scalars(stage, peer, count, me):
        copies = []
        for off in range(1, count):
            copy = pltpu.make_async_remote_copy(
                src_ref=sbuf.at[stage, me],
                dst_ref=sbuf.at[stage, me],
                send_sem=sc_send.at[stage, off],
                recv_sem=sc_recv.at[stage, off],
                device_id=peer(off),
                device_id_type=MESH,
            )
            copy.start()
            copies.append(copy)
        return copies

    def take_scalars(stage, copies):
        for copy in copies:
            copy.wait()
        total = sbuf[stage, 0]
        for index in range(1, len(copies) + 1):
            total = total + sbuf[stage, index]
        return total

    def send_ghosts(it):
        copies = []
        for index in order:
            delta = deltas[index]
            far = index == 4 and it > 0
            count = 1 if far else NBD
            copy = pltpu.make_async_remote_copy(
                src_ref=far_out if far else nd3.at[pl.ds(0, NBD)],
                dst_ref=cand.at[pl.ds(it * 24 + (index + 1) * NBD, count)],
                send_sem=gh_send.at[it, index],
                recv_sem=gh_recv.at[it, index],
                device_id=r_peer(regions - delta),
                device_id_type=MESH,
            )
            copy.start()
            copies.append(copy)
        return copies

    blocks_of = arc_blocks // CHUNKS

    def convert(chunk, first=0, end=blocks_of):
        if first == 0:
            inc_copies[chunk].wait()

        def step(index, carry):
            a = chunk * blocks_of + index
            for b in range(BPA):
                high, low = split(inc_buf[a * BPA + b])
                w2[a, b * BLK : (b + 1) * BLK, 0:BLK] = high
                w2[a, b * BLK : (b + 1) * BLK, BLK:] = low
            return carry

        lax.fori_loop(first, end, step, 0)

    scalar_copies = send_scalars(0, comm_peer, comms, c)
    ghost_copies = send_ghosts(0)
    arg_copies["gs"].wait()
    arg_copies["bn_row"].wait()
    ghost_at = []
    ghost_later = []
    code = bn_row[...]
    slots = code
    for g in range(NG):
        source = gs[g]
        block = source & (NBD - 1)
        delta = lax.rem((source >> 2) - r + regions, regions)
        behind = jnp.maximum(delta - (regions - 5), 3)
        relation = jnp.where(delta <= 2, delta, jnp.where(delta == regions // 2, 5, behind))
        ghost_at.append(relation * NBD + block)
        ghost_later.append(jnp.where(relation == 5, 5 * NBD, relation * NBD + block))
        row = jnp.where(
            relation == 0, block, jnp.where(relation == 5, own, own + block) + (relation - 1) * NBD
        )
        code = jnp.where(slots == own + g, row, code)
    hits = lax.broadcasted_iota(jnp.int32, (ROW_PAD, BLK), 0) == code
    one_hot = jnp.where(hits, 1.0, 0.0).astype(jnp.bfloat16)
    oh2[:, 0:BLK] = one_hot
    oh2[:, BLK:] = one_hot

    far_block = gs[0] & (NBD - 1)
    pick_out[...] = jnp.full(pick_out.shape, far_block, jnp.int32).astype(jnp.float32)

    for chunk in range(0, 2):
        convert(chunk)
    arg_copies["capacity"].wait()
    cap_sq = jnp.zeros((8, BLK), jnp.float32)
    for part in range(capacity.shape[0] // 8):
        piece = capacity[part * 8 : (part + 1) * 8]
        cap_sq = cap_sq + piece * piece
    pick_copy = pltpu.make_async_remote_copy(
        src_ref=pick_out,
        dst_ref=pick_in,
        send_sem=pick_send.at[0],
        recv_sem=pick_recv.at[0],
        device_id=r_peer(regions // 2),
        device_id_type=MESH,
    )
    pick_copy.start()
    total = take_scalars(0, scalar_copies)
    sbuf[1, x, 0:8] = total[0:8]
    sbuf[1, x, 8:16] = total[8:16] + cap_sq
    convert(2, 0, 1)
    scalar_copies = send_scalars(1, x_peer, x_size, x)
    convert(2, 1)
    for chunk in range(3, 5):
        convert(chunk)
    total = take_scalars(1, scalar_copies)
    sbuf[2, z] = total
    convert(5, 0, 1)
    scalar_copies = send_scalars(2, z_peer, Z_SIZE, z)
    convert(5, 1)
    for chunk in range(6, 8):
        convert(chunk)

    arg_copies["bn"].wait()
    arg_copies["cap_dual"].wait()
    arg_copies["flow"].wait()

    primal_step = None
    dual_step = None
    for it in range(ITERS):
        last = it == ITERS - 1
        flow_src = flow if it == 0 else flow_o
        cap_src = cap_dual if it == 0 else cap_o

        for copy in ghost_copies:
            copy.wait()
        for g in range(NG):
            high, low = split(cand[it * 24 + (ghost_later if it else ghost_at)[g]])
            dtab[own + g, 0:commodities] = high
            dtab[own + g, commodities:] = low

        def back_of(a):
            left = dtab[bn[a * BPA]]
            right = dtab[bn[a * BPA + 1]]
            product = jnp.dot(
                jnp.concatenate([left, right], axis=1),
                w2[a],
                preferred_element_type=jnp.float32,
            )
            half = product[:commodities] + product[commodities:]
            return half[:, :BLK] + half[:, BLK:]

        def update(a, back):
            now = flow_src[:, columns(a)]
            price = cost[:, columns(a)] - back + cap_src[pl.ds(a, 1), :]
            new = jnp.maximum(now - primal_step * price, 0.0)
            bar = 2.0 * new - now
            flow_o[:, columns(a)] = new
            load_s[pl.ds(a, 1), :] = jnp.sum(bar, axis=0, keepdims=True)
            back_s[:, columns(a)] = bar

        def back_step(index, carry):
            for part in range(UNROLL):
                a = index * UNROLL + part
                back_s[:, columns(a)] = back_of(a)
            return carry

        def update_step(index, carry):
            for part in range(UNROLL):
                a = index * UNROLL + part
                update(a, back_s[:, columns(a)])
            return carry

        def both_step(index, carry):
            for part in range(UNROLL):
                a = index * UNROLL + part
                update(a, back_of(a))
            return carry

        if it == 0:
            lax.fori_loop(0, arc_blocks // UNROLL, back_step, 0)
            total = take_scalars(2, scalar_copies)
            cost_all = jnp.sum(total[0:8], axis=(0, 1), keepdims=True)
            rest_all = jnp.sum(total[8:16], axis=(0, 1), keepdims=True)
            weight = jnp.sqrt(cost_all / rest_all)
            primal_step = jnp.broadcast_to(step_scale / weight, (1, BLK))
            dual_step = jnp.broadcast_to(step_scale * weight, (1, BLK))
            lax.fori_loop(0, arc_blocks // UNROLL, update_step, 0)
        else:
            lax.fori_loop(0, arc_blocks // UNROLL, both_step, 0)

        load_copies = []
        for off in range(1, comms):
            target = lax.rem(c + off, comms)
            copy = pltpu.make_async_remote_copy(
                src_ref=load_s.at[
                    pl.ds(pl.multiple_of(target * load_rows, load_rows), load_rows)
                ],
                dst_ref=ld_a.at[it, c],
                send_sem=ld_send.at[it, 0, off],
                recv_sem=ld_recv.at[it, 0, off],
                device_id=comm_peer(off),
                device_id_type=MESH,
            )
            copy.start()
            load_copies.append(copy)

        def forward_step(index, carry):
            for part in range(UNROLL):
                a = index * UNROLL + part
                high, low = split(back_s[:, columns(a)])
                terms = jnp.concatenate(
                    [
                        jnp.concatenate([high, high], axis=1),
                        jnp.concatenate([low, low], axis=1),
                    ],
                    axis=0,
                )
                product = lax.dot_general(
                    terms,
                    w2[a],
                    (((1,), (1,)), ((), ())),
                    preferred_element_type=jnp.float32,
                )
                half = product[:commodities] + product[commodities:]
                row = pl.multiple_of(a * (BPA * commodities), BPA * commodities)
                fwd[pl.ds(row, commodities), :] = half[:, :BLK]
                fwd[pl.ds(row + commodities, commodities), :] = half[:, BLK:]
            return carry

        lax.fori_loop(0, arc_blocks // UNROLL, forward_step, 0)

        blocks = BPA * arc_blocks
        for pair in range(commodities // 2):
            high_0, low_0 = split(fwd[pl.ds(2 * pair, blocks, stride=commodities), :])
            high_1, low_1 = split(fwd[pl.ds(2 * pair + 1, blocks, stride=commodities), :])
            terms = jnp.concatenate(
                [
                    jnp.concatenate([high_0, high_1], axis=1),
                    jnp.concatenate([low_0, low_1], axis=1),
                ],
                axis=0,
            )
            rows = jnp.dot(oh2[...], terms, preferred_element_type=jnp.float32)
            slot[pl.ds(2 * pair, ROW_PAD, stride=commodities), :] = rows[:, :BLK]
            slot[pl.ds(2 * pair + 1, ROW_PAD, stride=commodities), :] = rows[:, BLK:]

        def updated(s, rows):
            return nd3[s] + dual_step * (demand[:, columns(s)] - rows)

        def keep(s, value):
            if last:
                nd_o[:, columns(s)] = value
            else:
                nd3[s] = value
                high, low = split(value)
                dtab[s, 0:commodities] = high
                dtab[s, commodities:] = low

        def inner_step(index, carry):
            for part in range(4):
                s = NBD + index * 4 + part
                row = pl.multiple_of(s * commodities, commodities)
                keep(s, updated(s, slot[pl.ds(row, commodities), :]))
            return carry

        lax.fori_loop(0, 1, inner_step, 0)

        routed_copies = []
        for index in order:
            delta = deltas[index]
            rows = NBD * commodities
            count = commodities if index == 4 else rows
            copy = pltpu.make_async_remote_copy(
                src_ref=slot.at[pl.ds(own * commodities + index * rows, count)],
                dst_ref=rbuf.at[it, index, pl.ds(0, count)],
                send_sem=rt_send.at[it, index],
                recv_sem=rt_recv.at[it, index],
                device_id=r_peer(delta),
                device_id_type=MESH,
            )
            copy.start()
            routed_copies.append(copy)

        for copy in load_copies:
            copy.wait()
        mine = load_s[pl.ds(pl.multiple_of(c * load_rows, load_rows), load_rows), :]
        for off in range(1, comms):
            mine = mine + ld_a[it, lax.rem(c + off, comms)]
        ld_b[it, c] = mine

        lax.fori_loop(1, (own - NBD) // 4, inner_step, 0)

        total_copies = []
        for off in range(1, comms):
            copy = pltpu.make_async_remote_copy(
                src_ref=ld_b.at[it, c],
                dst_ref=ld_b.at[it, c],
                send_sem=ld_send.at[it, 1, off],
                recv_sem=ld_recv.at[it, 1, off],
                device_id=comm_peer(off),
                device_id_type=MESH,
            )
            copy.start()
            total_copies.append(copy)

        def finish_load(at, copies=total_copies, source=cap_src):
            for copy in copies:
                copy.wait()
            for owner in range(comms):
                rows = slice(owner * load_rows, (owner + 1) * load_rows)
                excess = ld_b[at, owner] - capacity[rows]
                cap_o[rows] = jnp.maximum(source[rows] + dual_step * excess, 0.0)

        if it == 0:
            pick_copy.wait()
        picked = pick_in[...]
        for copy in routed_copies:
            copy.wait()
        far_value = jnp.zeros((commodities, BLK), jnp.float32)
        for j in range(NBD):
            rows = slot[j * commodities : (j + 1) * commodities, :]
            for index in range(4):
                rows = rows + rbuf[it, index, j * commodities : (j + 1) * commodities, :]
            rows = rows + jnp.where(picked == float(j), rbuf[it, 4, 0:commodities, :], 0.0)
            value = updated(j, rows)
            keep(j, value)
            if not last:
                cand[(it + 1) * 24 + j] = value
                far_value = jnp.where(picked == float(j), value, far_value)
        if not last:
            far_out[0] = far_value
        if last:
            finish_load(it)
        else:
            ghost_copies = send_ghosts(it + 1)
            finish_load(it)


def settle(count, *refs):
    sources, targets, sem = refs[:count], refs[count : 2 * count], refs[2 * count]
    leaving = []
    for index in range(count):
        rows = sources[index].shape[0] // 2
        for part in range(2):
            at = pl.ds(part * rows, rows)
            copy = pltpu.make_async_copy(
                sources[index].at[at], targets[index].at[at], sem.at[index, part]
            )
            copy.start()
            leaving.append(copy)
    for copy in leaving:
        copy.wait()


def body(
    cost,
    flow_start,
    capacity,
    cap_dual_start,
    demand,
    node_dual_start,
    incidence,
    block_node,
    ghost_source,
):
    regions = lax.axis_size("region")
    comms = lax.axis_size("comm")
    commodities, arcs = cost.shape
    nodes = demand.shape[1]
    arc_blocks = arcs // BLK
    own = nodes // BLK
    blocks = incidence.shape[0]
    f32, bf16 = jnp.float32, jnp.bfloat16
    hbm = pl.BlockSpec(memory_space=pltpu.HBM)
    vmem = pl.BlockSpec(memory_space=pltpu.VMEM)
    dma = pltpu.SemaphoreType.DMA
    relations = 5
    flow_end, cap_end, node_end = pl.pallas_call(
        functools.partial(kernel, regions, comms),
        name="pdhg",
        out_shape=(
            jax.ShapeDtypeStruct((commodities, arcs), f32),
            jax.ShapeDtypeStruct((arc_blocks, BLK), f32),
            jax.ShapeDtypeStruct((commodities, nodes), f32),
        ),
        in_specs=[hbm] * 10,
        out_specs=(vmem, vmem, vmem),
        scratch_shapes=[
            pltpu.SMEM((blocks,), jnp.int32),
            pltpu.SMEM((NG,), jnp.int32),
            pltpu.VMEM((1, blocks), jnp.int32),
            pltpu.VMEM((commodities, arcs), f32),
            pltpu.VMEM((commodities, arcs), f32),
            pltpu.VMEM((arc_blocks, BLK), f32),
            pltpu.VMEM((arc_blocks, BLK), f32),
            pltpu.VMEM((commodities, nodes), f32),
            pltpu.VMEM((commodities, nodes), f32),
            pltpu.VMEM((blocks, BLK, BLK), f32),
            pltpu.VMEM((arc_blocks, BPA * BLK, 2 * BLK), bf16),
            pltpu.VMEM((commodities, arcs), f32),
            pltpu.VMEM((own, commodities, BLK), f32),
            pltpu.VMEM((own + NG, 2 * commodities, BLK), bf16),
            pltpu.VMEM((ROW_PAD, 2 * BLK), bf16),
            pltpu.VMEM((ITERS * 24, commodities, BLK), f32),
            pltpu.VMEM((blocks * commodities, BLK), f32),
            pltpu.VMEM((ROW_PAD * commodities, BLK), f32),
            pltpu.VMEM((ITERS, relations, NBD * commodities, BLK), f32),
            pltpu.VMEM((arc_blocks, BLK), f32),
            pltpu.VMEM((ITERS, comms, arc_blocks // comms, BLK), f32),
            pltpu.VMEM((ITERS, comms, arc_blocks // comms, BLK), f32),
            pltpu.VMEM((3, 8, 16, BLK), f32),
            pltpu.VMEM((commodities, BLK), f32),
            pltpu.VMEM((commodities, BLK), f32),
            pltpu.VMEM((1, commodities, BLK), f32),
            dma((1,)),
            dma((1,)),
            dma((9,)),
            dma((CHUNKS,)),
            dma((3, 8)),
            dma((3, 8)),
            dma((ITERS, relations)),
            dma((ITERS, relations)),
            dma((ITERS, relations)),
            dma((ITERS, relations)),
            dma((ITERS, 2, 8)),
            dma((ITERS, 2, 8)),
        ],
        compiler_params=pltpu.CompilerParams(
            collective_id=0, has_side_effects=True, vmem_limit_bytes=50_000_000
        ),
    )(
        *(
            pltpu.with_memory_space_constraint(value, pltpu.HBM)
            for value in (
                block_node,
                ghost_source,
                block_node.reshape(1, blocks),
                cost,
                flow_start,
                capacity.reshape(arc_blocks, BLK),
                cap_dual_start.reshape(arc_blocks, BLK),
                demand,
                node_dual_start,
                incidence,
            )
        )
    )
    shapes = (flow_end.shape, cap_end.shape, node_end.shape)
    flow_end, cap_end, node_end = pl.pallas_call(
        functools.partial(settle, 3),
        name="settle",
        out_shape=tuple(jax.ShapeDtypeStruct(shape, f32) for shape in shapes),
        in_specs=[vmem] * 3,
        out_specs=(hbm, hbm, hbm),
        scratch_shapes=[dma((3, 2))],
        compiler_params=pltpu.CompilerParams(vmem_limit_bytes=1024 * 1024),
    )(flow_end, cap_end, node_end)
    return flow_end, cap_end.reshape(arcs), node_end


def solution(mesh):
    return jax.shard_map(
        body,
        mesh=mesh,
        in_specs=(
            P("comm", "region"),
            P("comm", "region"),
            P("region"),
            P("region"),
            P("comm", "region"),
            P("comm", "region"),
            P("region", None, None),
            P("region"),
            P("region"),
        ),
        out_specs=(P("comm", "region"), P("region"), P("comm", "region")),
        check_vma=False,
    )
```
